256 devices in a mesh: rep: 16 (over z_lo, y), gx: 8 (over x, core), gy: 2 (over z_hi).
Axes of the slice: x: 4, y: 4, z: 8 (z_hi: 2, z_lo: 4; z = z_hi * 4 + z_lo), core: 2. Of those that a mesh axis runs over, the one named last changes fastest.
Arguments:
- particle_descriptors: bfloat16 [16, 16, 4, 128, 128], P('rep', 'gx', 'gy'), may hold values from -6 to 6
- particle_locations_all: float32 [16, 3, 16, 4, 128], P('rep', None, 'gx', 'gy'), may hold values from 0 to 16, as said below
- earlier_jitter: float32 [16, 3, 16, 4, 128], P('rep', None, 'gx', 'gy'), may hold values from -6 to 6
- later_jitter: float32 [16, 3, 16, 4, 128], P('rep', None, 'gx', 'gy'), may hold values from -6 to 6
- adjacent_tile_slots: int32 [16, 4, 6], P('gx', 'gy'), may hold values from -1 to 15, as said below
- thermal_levels: float32 [16], replicated, may hold values from 0.5 to 2
- heat_slot_of_copy: int32 [16], P('rep'), may hold values from 0 to 15, as said below
- partner_choice: int32 [16], replicated, may hold values from 0 to 15, as said below
- normalizer_gain: float32 [128], replicated, may hold values from 0.25 to 1.75
- query_lookup_matrix: bfloat16 [128, 384], replicated, may hold values from -0.5 to 0.5
- message_output_matrix: bfloat16 [128, 128], replicated, may hold values from -0.5 to 0.5
- lookup_charge_map: bfloat16 [128], replicated, may hold values from -0.5 to 0.5
- attention_head_falloff: float32 [8], replicated, may hold values from 0.5 to 8
- attention_head_weight: float32 [8], replicated, may hold values from -4 to 4
Outputs:
- interval_descriptors: bfloat16 [16, 16, 4, 128, 128], P('rep', 'gx', 'gy')
- interval_locations: float32 [16, 3, 16, 4, 128], P('rep', None, 'gx', 'gy')
- later_pulls: float32 [16, 3, 16, 4, 128], P('rep', None, 'gx', 'gy')
The draws below stay inside these ranges and needn't reach their ends.
Inputs may be any that keep to these rules, and one draw needn't show every extreme that they name: `adjacent_tile_slots`: each tile's first slot names the tile itself; the others name distinct tiles of the 3 x 3 block of tiles around it that lie inside the grid, as row-major indices into the device's block of tiles extended by one tile on each side (4 columns); -1 marks an empty slot, and empty slots come last. `heat_slot_of_copy`: A permutation. `partner_choice`: an involution: each replica takes its own configuration or that of the replica whose temperature slot is next to its own. `particle_locations_all`: for a bead of the tile at grid position (a, b) the first coordinate lies in [a, a + 1], the second in [b, b + 1], the third in [0, 1].
All inputs are finite; a program needn't handle non-finite values.
Results may differ from the reference program's by a relative error of at most 0.0091.
Values may be sent and summed in bfloat16 or wider, within the bound.
No kernel may reach another device: no remote copies, remote signals or barrier semaphores. Data moves between devices by JAX's collectives and lax.ppermute only.
A program may use at most 64 MiB of HBM per device.

```python
import math
import jax
import jax.numpy as jnp
from jax import lax

F = 128
HEADS = 8
TILE = 128
K = 6
TX = 2
TY = 2
NREP = 16
GTX = 16
GTY = 4


def draw_particle_locations_all(key, part):
    array_shape = (NREP, 3, GTX, GTY, TILE)
    fraction = jax.random.uniform(key, array_shape, jnp.float32)
    component = jnp.arange(3)[None, :, None, None, None]
    grid_row = jnp.arange(GTX, dtype=jnp.float32)[None, None, :, None, None]
    grid_col = jnp.arange(GTY, dtype=jnp.float32)[None, None, None, :, None]
    anchor = jnp.where(component == 0, grid_row, jnp.where(component == 1, grid_col, 0.0))
    return anchor + fraction


def draw_adjacent_tile_slots(key, part):
    step_row = jnp.array([-1, -1, -1, 0, 0, 1, 1, 1], dtype=jnp.int32)
    step_col = jnp.array([-1, 0, 1, -1, 1, -1, 0, 1], dtype=jnp.int32)
    grid_row = jnp.arange(GTX, dtype=jnp.int32)[:, None, None]
    grid_col = jnp.arange(GTY, dtype=jnp.int32)[None, :, None]
    target_row = grid_row + step_row
    target_col = grid_col + step_col
    inside = (target_row >= 0) & (target_row < GTX) & (target_col >= 0) & (target_col < GTY)
    ranking = jax.random.randint(key, (GTX, GTY, 8), 0, 2 ** 20, dtype=jnp.int32) * 16 + jnp.arange(8, dtype=jnp.int32)
    ranking = jnp.where(inside, ranking, ranking + 2 ** 26)
    picked = jnp.argsort(ranking, axis=-1)[..., :K - 1]
    chosen_row = step_row[picked]
    chosen_col = step_col[picked]
    chosen_inside = jnp.take_along_axis(inside, picked, axis=-1)
    local_row = grid_row % TX + 1
    local_col = grid_col % TY + 1
    others = (local_row + chosen_row) * (TY + 2) + local_col + chosen_col
    others = jnp.where(chosen_inside, others, -1)
    itself = jnp.broadcast_to(local_row * (TY + 2) + local_col, (GTX, GTY, 1))
    return jnp.concatenate([itself, others], axis=-1).astype(jnp.int32)


def replica_ladder(key):
    base_key = jax.random.fold_in(key, 31)
    first_key, second_key, third_key = jax.random.split(base_key, 3)
    slot_of = jax.random.permutation(first_key, NREP).astype(jnp.int32)
    holder = jnp.argsort(slot_of).astype(jnp.int32)
    parity = jax.random.randint(second_key, (), 0, 2, dtype=jnp.int32)
    accepted = jax.random.randint(third_key, (NREP,), 0, 4, dtype=jnp.int32) > 0
    slot_ids = jnp.arange(NREP, dtype=jnp.int32)
    shifted = slot_ids - parity
    goes_up = (shifted >= 0) & (shifted % 2 == 0) & (slot_ids + 1 < NREP)
    goes_down = (shifted >= 1) & (shifted % 2 == 1)
    pair_number = jnp.clip(jnp.where(goes_up, shifted // 2, (shifted - 1) // 2), 0, NREP - 1)
    accepted_pair = accepted[pair_number]
    partner = jnp.where(goes_up & accepted_pair, slot_ids + 1, jnp.where(goes_down & accepted_pair, slot_ids - 1, slot_ids))
    return (slot_of, holder[partner[slot_of]].astype(jnp.int32))


def draw_heat_slot_of_copy(key, part):
    slot_of, partners = replica_ladder(key)
    return slot_of


def draw_partner_choice(key, part):
    slot_of, partners = replica_ladder(key)
    return partners


def levels(stream_key, extent, cuts, low, largest):
    def one(dim, parts):
        heights = jax.random.uniform(jax.random.fold_in(jax.random.fold_in(stream_key, 6), dim), (parts,), jnp.float32, low / len(cuts), largest / len(cuts))
        return jnp.repeat(jnp.exp(heights), extent[dim] // parts).reshape((-1,) + (1,) * (len(extent) - dim - 1))

    loudness = one(*cuts[0])
    for cut in cuts[1:]:
        loudness = loudness * one(*cut)
    return loudness


def normal_values(key, shape, deviation, limit, shards=(), kind=jnp.bfloat16):
    loudness = levels(key, shape, shards, -0.22, 0.18) if shards else 1.0
    entries = jax.random.normal(key, shape, jnp.float32) * deviation * loudness
    return jnp.minimum(jnp.maximum(entries, -limit), limit).astype(kind)


def setup_inputs(seed: int = 0) -> dict:
    keys = jax.random.split(jax.random.key(seed), 15)
    return {
        "particle_descriptors": normal_values(keys[0], (NREP, GTX, GTY, TILE, F), 1.0, 6.0, ((0, 16), (1, 8), (2, 2))),
        "particle_locations_all": draw_particle_locations_all(jax.random.fold_in(keys[14], 71), 0),
        "earlier_jitter": normal_values(keys[2], (NREP, 3, GTX, GTY, TILE), 1.0, 6.0, ((0, 16), (2, 8), (3, 2)), jnp.float32),
        "later_jitter": normal_values(keys[3], (NREP, 3, GTX, GTY, TILE), 1.0, 6.0, ((0, 16), (2, 8), (3, 2)), jnp.float32),
        "adjacent_tile_slots": draw_adjacent_tile_slots(jax.random.fold_in(keys[14], 71), 0),
        "thermal_levels": jnp.clip(jnp.exp(jax.random.uniform(keys[5], (NREP,), jnp.float32, math.log(0.5), math.log(2.0))), 0.5, 2.0),
        "heat_slot_of_copy": draw_heat_slot_of_copy(jax.random.fold_in(keys[14], 71), 0),
        "partner_choice": draw_partner_choice(jax.random.fold_in(keys[14], 71), 0),
        "normalizer_gain": jnp.clip(1.0 + 0.15 * jax.random.normal(keys[8], (F,), jnp.float32), 0.25, 1.75),
        "query_lookup_matrix": normal_values(keys[9], (F, 3 * F), F ** -0.5, 0.5),
        "message_output_matrix": normal_values(keys[10], (F, F), F ** -0.5, 0.5),
        "lookup_charge_map": normal_values(keys[11], (F,), F ** -0.5, 0.5),
        "attention_head_falloff": jnp.clip(jnp.exp(jax.random.uniform(keys[12], (HEADS,), jnp.float32, math.log(0.5), math.log(8.0))), 0.5, 8.0),
        "attention_head_weight": normal_values(keys[13], (HEADS,), 1.0, 4.0, (), jnp.float32),
    }


NORM_EPS = 1e-05
DURATION_DELTA = 0.1
JITTER_SIZE = 0.05
MESSAGE_SCALE = 1.0 / 32.0
FORCE_SCALE = 1.0 / 16.0

def layer_norm(latent_vector, normalizer_gain):
    values = latent_vector.astype(jnp.float32)
    center = lax.optimization_barrier(jnp.mean(values, axis=-1, keepdims=True))
    spread = lax.optimization_barrier(jnp.mean((values - center) ** 2, axis=-1, keepdims=True))
    return ((values - center) * lax.rsqrt(spread + NORM_EPS) * normalizer_gain).astype(jnp.bfloat16)

def tile_terms(query_rows, own_coords, keyval, probe_values, near_coords, occupied_flags, attention_head_falloff, attention_head_weight):
    bead_count, feature_count = query_rows.shape
    head_count = attention_head_falloff.shape[0]
    head_size = feature_count // head_count
    slot_count = keyval.shape[0]
    queries = query_rows.astype(jnp.float32).reshape(bead_count, head_count, head_size)
    keys_heads = keyval[..., :feature_count].astype(jnp.float32).reshape(slot_count, bead_count, head_count, head_size)
    values_heads = keyval[..., feature_count:].astype(jnp.float32).reshape(slot_count, bead_count, head_count, head_size)
    logits = jnp.einsum('ihd,njhd->hinj', queries, keys_heads)
    offsets = own_coords[:, :, None, None] - near_coords[:, None, :, :]
    squared = lax.optimization_barrier(jnp.sum(offsets * offsets, axis=0))
    radius = jnp.sqrt(squared)
    envelope = jnp.where(radius < 1.0, 0.5 * (jnp.cos(jnp.pi * radius) + 1.0), 0.0)
    envelope = envelope * occupied_flags.astype(jnp.float32)[None, :, None]
    scores = jax.nn.silu(logits / math.sqrt(head_size)) * envelope[None] * jnp.exp(-attention_head_falloff[:, None, None, None] * squared[None])
    rounded = lax.optimization_barrier(scores.astype(jnp.bfloat16)).astype(jnp.float32)
    message = jnp.einsum('hinj,njhd->ihd', rounded, values_heads) * MESSAGE_SCALE
    message = message.reshape(bead_count, feature_count).astype(jnp.bfloat16)
    mixing = lax.optimization_barrier(jnp.sum(attention_head_weight[:, None, None, None] * scores, axis=0))
    particle_pulls = lax.optimization_barrier(jnp.sum(offsets * (mixing * probe_values[None, :, :])[None], axis=(2, 3))) * FORCE_SCALE
    return (message, particle_pulls)

def global_slots(adjacent_tile_slots):
    occupied_flags = adjacent_tile_slots >= 0
    clipped = jnp.maximum(adjacent_tile_slots, 0)
    grid_row = jnp.arange(GTX, dtype=jnp.int32)[:, None, None]
    grid_col = jnp.arange(GTY, dtype=jnp.int32)[None, :, None]
    padded_row = grid_row - grid_row % TX + clipped // (TY + 2)
    padded_col = grid_col - grid_col % TY + clipped % (TY + 2)
    linear_offset = (padded_row * (GTY + 2) + padded_col).astype(jnp.int32)
    return (linear_offset.reshape(-1, K), occupied_flags.reshape(-1, K))

def propagate_copy(latent_vector, particle_locations, stochastic_jolts, copy_heat_level, linear_offset, occupied_flags, network_weights):
    normalizer_gain, query_lookup_matrix, message_output_matrix, lookup_charge_map, attention_head_falloff, attention_head_weight = network_weights
    grid_rows, grid_cols, tile_beads, feature_count = latent_vector.shape
    normed = layer_norm(latent_vector, normalizer_gain)
    projected = jnp.dot(normed.reshape(-1, feature_count), query_lookup_matrix, preferred_element_type=jnp.float32).astype(jnp.bfloat16)
    query_rows = projected[:, :feature_count].reshape(-1, tile_beads, feature_count)
    keyval = projected[:, feature_count:].reshape(grid_rows, grid_cols, tile_beads, 2 * feature_count)
    keyval = jnp.pad(keyval, ((1, 1), (1, 1), (0, 0), (0, 0))).reshape(-1, tile_beads, 2 * feature_count)
    probe_values = jnp.dot(keyval[..., :feature_count].reshape(-1, feature_count), lookup_charge_map, preferred_element_type=jnp.float32).reshape(-1, tile_beads)
    near_coords = jnp.pad(particle_locations, ((0, 0), (1, 1), (1, 1), (0, 0))).reshape(3, -1, tile_beads)
    own_coords = particle_locations.reshape(3, -1, tile_beads).transpose(1, 0, 2)

    def per_tile(tile_item):
        tile_query, tile_coords, tile_slots, tile_present = tile_item
        return tile_terms(tile_query, tile_coords, keyval[tile_slots], probe_values[tile_slots], near_coords[:, tile_slots], tile_present, attention_head_falloff, attention_head_weight)
    message, particle_pulls = lax.map(per_tile, (query_rows, own_coords, linear_offset, occupied_flags))
    mixed = jnp.dot(message.reshape(-1, feature_count), message_output_matrix, preferred_element_type=jnp.float32).reshape(latent_vector.shape)
    revised_latent = (latent_vector.astype(jnp.float32) + mixed).astype(jnp.bfloat16)
    particle_pulls = particle_pulls.transpose(1, 0, 2).reshape(particle_locations.shape)
    moved_locations = particle_locations + DURATION_DELTA * particle_pulls + JITTER_SIZE * jnp.sqrt(copy_heat_level) * stochastic_jolts
    return (revised_latent, moved_locations, particle_pulls)

def reference(particle_descriptors, particle_locations_all, earlier_jitter, later_jitter, adjacent_tile_slots, thermal_levels, heat_slot_of_copy, partner_choice, normalizer_gain, query_lookup_matrix, message_output_matrix, lookup_charge_map, attention_head_falloff, attention_head_weight):
    network_weights = (normalizer_gain, query_lookup_matrix, message_output_matrix, lookup_charge_map, attention_head_falloff, attention_head_weight)
    linear_offset, occupied_flags = global_slots(adjacent_tile_slots)
    heat_level_series = jnp.take(thermal_levels, heat_slot_of_copy)

    def earlier_move(copy_element):
        latent_vector, particle_locations, stochastic_jolts, copy_heat_level = copy_element
        revised_latent, moved_locations, ignored_output = propagate_copy(latent_vector, particle_locations, stochastic_jolts, copy_heat_level, linear_offset, occupied_flags, network_weights)
        return (revised_latent, moved_locations)
    starting_latent, starting_locations = lax.map(earlier_move, (particle_descriptors, particle_locations_all, earlier_jitter, heat_level_series))
    traded_latent = jnp.take(starting_latent, partner_choice, axis=0)
    traded_locations = jnp.take(starting_locations, partner_choice, axis=0)

    def later_move(copy_element):
        latent_vector, particle_locations, stochastic_jolts, copy_heat_level = copy_element
        return propagate_copy(latent_vector, particle_locations, stochastic_jolts, copy_heat_level, linear_offset, occupied_flags, network_weights)
    interval_descriptors, interval_locations, later_pulls = lax.map(later_move, (traded_latent, traded_locations, later_jitter, heat_level_series))
    return (interval_descriptors, interval_locations, later_pulls)
```

```python
import math

import jax
import jax.numpy as jnp
from jax import lax
from jax.experimental import pallas as pl
from jax.experimental.pallas import tpu as pltpu
from jax.sharding import PartitionSpec as P

F = 128
HEADS = 8
HD = 16
T = 128
K = 6
PR = T + 16
XR = 40
NORM_EPS = 1e-05
DELTA = 0.1
JITTER = 0.05
MESSAGE_SCALE = 1.0 / 32.0
FORCE_SCALE = 1.0 / 16.0
LOG2E = 1.4426950408889634
INTERPRET = False

BF = jnp.bfloat16
F32 = jnp.float32


def cos_half_coefs():
    return [(-1) ** k * (math.pi / 2) ** (2 * k) / math.factorial(2 * k) for k in range(8)]


def call(body, name, out_shape, in_specs, scratch=()):
    return pl.pallas_call(
        body,
        name=name,
        out_shape=out_shape,
        in_specs=in_specs,
        scratch_shapes=scratch,
        interpret=INTERPRET,
    )


def vm():
    return pl.BlockSpec(memory_space=pltpu.VMEM)


def sm():
    return pl.BlockSpec(memory_space=pltpu.SMEM)


def parts3(x):
    hi = x.astype(BF).astype(F32)
    rest = x - hi
    mid = rest.astype(BF).astype(F32)
    lo = rest - mid
    return hi, mid, lo


def norm_rows(h, gain):
    x = h.astype(F32)
    mean = jnp.mean(x, axis=-1, keepdims=True)
    xc = x - mean
    var = jnp.mean(xc * xc, axis=-1, keepdims=True)
    return (xc * lax.rsqrt(var + NORM_EPS) * gain).astype(BF)


def emit_rows(side, tiles, coords, r0, r1, g, cbuf):
    blocks = []
    for t in range(4):
        cbuf[t] = jnp.zeros((16, T), F32)
        for c in range(3):
            for k, part in enumerate(parts3(coords(c, t))):
                cbuf[t, c * 3 + k : c * 3 + k + 1, :] = part
        blocks.append(cbuf[t].astype(BF))
    for t in range(4):
        dst = r0 if t < 2 else r1
        dst[t % 2, 0:T, :] = tiles[t]
        dst[t % 2, T:PR, :] = blocks[t]
    for la in range(2):
        pick = side == 0
        g[la, 0:T, :] = jnp.where(pick, tiles[2 * la + 1], tiles[2 * la])
        g[la, T:PR, :] = jnp.where(pick, blocks[2 * la + 1], blocks[2 * la])


def first_body(side, h, p, gain, r0, r1, g, cbuf):
    tiles = [norm_rows(h[t * T : (t + 1) * T, :], gain[...]) for t in range(4)]
    emit_rows(side[0], tiles, lambda c, t: p[c * 4 + t : c * 4 + t + 1, :], r0, r1, g, cbuf)


def second_body(side, x, gain, r0, r1, g, h, p, cbuf):
    tiles = []
    for t in range(4):
        for c in range(3):
            blk = x[4 * t + c, 32:40, :].astype(F32)
            p[c * 4 + t : c * 4 + t + 1, :] = blk[0:1] + blk[1:2] + blk[2:3]
        for q in range(4):
            h[t * T + q * 32 : t * T + (q + 1) * 32, :] = x[4 * t + q, 0:32, :]
        tiles.append(norm_rows(h[t * T : (t + 1) * T, :], gain[...]))
    emit_rows(side[0], tiles, lambda c, t: p[c * 4 + t : c * 4 + t + 1, :], r0, r1, g, cbuf)


def head_mask(e):
    lane = lax.broadcasted_iota(jnp.int32, (T, F), 1)
    return (lane >= e * HD) & (lane < (e + 1) * HD)


def project_kv(tile, n, wkv, charge, kbuf, vbuf, pbuf):
    kv = jnp.dot(tile, wkv, preferred_element_type=F32)
    k = kv[:, :F].astype(BF)
    kbuf[n] = k
    v = kv[:, F:]
    for e in range(HEADS):
        vbuf[n, e * T : (e + 1) * T, :] = jnp.where(head_mask(e), v, 0.0).astype(BF)
    pbuf[n] = lax.dot_general(
        charge, k, (((1,), (1,)), ((), ())), preferred_element_type=F32
    )


def project_q(tile, wq, qbuf):
    q = jnp.dot(tile, wq, preferred_element_type=F32).astype(BF).astype(F32) * 0.125
    for e in range(HEADS):
        qbuf[e * T : (e + 1) * T, :] = jnp.where(head_mask(e), q, 0.0).astype(BF)


def pair_terms(m, n, falloff, headw, qbuf, kbuf, vbuf, pbuf, jbuf, ibuf, macc, facc):
    near = jbuf[n]
    mine = ibuf[m]
    d = [mine[:, c : c + 1] - near[c : c + 1, :] for c in range(3)]
    r2 = d[0] * d[0] + d[1] * d[1] + d[2] * d[2]
    coefs = cos_half_coefs()
    poly = jnp.full((T, T), coefs[-1], F32)
    for cf in coefs[-2::-1]:
        poly = poly * r2 + cf
    cut = jnp.where(r2 < 1.0, poly * poly, 0.0)
    k = kbuf[n]
    mix = jnp.zeros((T, T), F32)
    out = jnp.zeros((T, F), F32)
    for e2 in range(HEADS // 2):
        half = lax.dot_general(
            qbuf[e2 * 2 * T : (e2 + 1) * 2 * T, :],
            k,
            (((1,), (1,)), ((), ())),
            preferred_element_type=F32,
        )
        ws = []
        for s in range(2):
            e = e2 * 2 + s
            u = half[s * T : (s + 1) * T, :]
            decay = jnp.exp2(r2 * (falloff[e] * (-LOG2E))) * cut
            score = (u * (1.0 + jnp.tanh(u))) * decay
            mix = mix + score * headw[e]
            ws.append(score.astype(BF))
        out = out + jnp.dot(
            jnp.concatenate(ws, axis=1),
            vbuf[n, e2 * 2 * T : (e2 + 1) * 2 * T, :],
            preferred_element_type=F32,
        )
    macc[...] += out
    w = mix * pbuf[n, 0:1, :]
    for c in range(3):
        facc[c] += w * d[c]


def stored_index(slot, side):
    row = slot // 4
    col = slot - row * 4
    outer = (col == 0) | (col == 3)
    middle = (row == 1) | (row == 2)
    inner = jnp.where(middle, (row - 1) * 2 + (col - 1), jnp.where(row == 0, 3 + col, 5 + col))
    edge = jnp.where(middle, 7 + row, jnp.where(row == 0, 10, 11))
    return jnp.where(slot < 0, -1, jnp.where(outer, edge, inner))


def own_columns(p, ibuf, t):
    rows = jnp.concatenate(
        [p[c * 4 + t : c * 4 + t + 1, :] for c in range(3)] + [jnp.zeros((5, T), F32)], axis=0
    )
    ibuf[t] = rows.T
    return rows


def force_rows(facc):
    return [jnp.sum(facc[c].T, axis=0, keepdims=True) for c in range(3)]


def own_body(
    slots, falloff, headw, r0, r1, p, wqkv, charge, macc_out, frow_out,
    qbuf, kbuf, vbuf, pbuf, jbuf, ibuf, macc, facc,
):
    for t in range(4):
        src = r0 if t < 2 else r1
        project_kv(src[t % 2, 0:T, :], t, wqkv[:, F:], charge[...], kbuf, vbuf, pbuf)
        jbuf[t] = own_columns(p, ibuf, t)
    frow_out[...] = jnp.zeros((16, T), F32)
    for t in range(4):
        src = r0 if t < 2 else r1
        project_q(src[t % 2, 0:T, :], wqkv[:, :F], qbuf)
        macc[...] = jnp.zeros((T, F), F32)
        facc[...] = jnp.zeros((3, T, T), F32)

        def step(s, carry):
            n = stored_index(slots[t * K + s], 0)

            @pl.when((n >= 0) & (n < 4))
            def _():
                pair_terms(
                    t, n, falloff, headw, qbuf, kbuf, vbuf, pbuf, jbuf, ibuf, macc, facc
                )

            return carry

        lax.fori_loop(0, K, step, 0)
        macc_out[t * T : (t + 1) * T, :] = macc[...]
        for c, row in enumerate(force_rows(facc)):
            frow_out[t * 4 + c : t * 4 + c + 1, :] = row


def rest_body(
    last,
    slots, falloff, headw, levels, heat, r0, r1, p, h, jit, up, down, gin, c0, c1,
    macc_in, frow_in, wqkv, wo, charge,
    *refs,
):
    if last:
        hout, pout, fout = refs[:3]
        refs = refs[3:]
    else:
        xout = refs[0]
        refs = refs[1:]
    qbuf, kbuf, vbuf, pbuf, jbuf, ibuf, macc, facc = refs[:8]
    halo = [(up, 0), (up, 1), (down, 0), (down, 1), (gin, 0), (gin, 1), (c0, 0), (c1, 0)]
    for i, (src, a) in enumerate(halo):
        project_kv(src[a, 0:T, :], i, wqkv[:, F:], charge[...], kbuf, vbuf, pbuf)
        blk = src[a, T:PR, :].astype(F32)
        jbuf[i] = jnp.concatenate(
            [blk[3 * c : 3 * c + 1] + blk[3 * c + 1 : 3 * c + 2] + blk[3 * c + 2 : 3 * c + 3] for c in range(3)]
            + [jnp.zeros((5, T), F32)],
            axis=0,
        )
    scale = JITTER * jnp.sqrt(jnp.full((1, T), levels[heat[0]], F32))
    for t in range(4):
        src = r0 if t < 2 else r1
        own_columns(p, ibuf, t)
        project_q(src[t % 2, 0:T, :], wqkv[:, :F], qbuf)
        macc[...] = macc_in[t * T : (t + 1) * T, :]
        facc[...] = jnp.zeros((3, T, T), F32)

        def step(s, carry):
            n = stored_index(slots[t * K + s], 0)

            @pl.when(n >= 4)
            def _():
                pair_terms(
                    t, n - 4, falloff, headw, qbuf, kbuf, vbuf, pbuf, jbuf, ibuf, macc, facc
                )

            return carry

        lax.fori_loop(0, K, step, 0)
        message = (macc[...] * MESSAGE_SCALE).astype(BF)
        mixed = jnp.dot(message, wo[...], preferred_element_type=F32)
        updated = (h[t * T : (t + 1) * T, :].astype(F32) + mixed).astype(BF)
        if last:
            hout[t * T : (t + 1) * T, :] = updated
        else:
            for q in range(4):
                xout[4 * t + q, 0:32, :] = updated[q * 32 : (q + 1) * 32, :]
        for c, row in enumerate(force_rows(facc)):
            force = (row + frow_in[t * 4 + c : t * 4 + c + 1, :]) * FORCE_SCALE
            at = c * 4 + t
            moved = p[at : at + 1, :] + DELTA * force + scale * jit[at : at + 1, :]
            if last:
                pout[at : at + 1, :] = moved
                fout[at : at + 1, :] = force
            else:
                xout[4 * t + c, 32:40, :] = jnp.concatenate(
                    list(parts3(moved)) + [jnp.zeros((5, T), F32)], axis=0
                ).astype(BF)
        if not last:
            xout[4 * t + 3, 32:40, :] = jnp.zeros((8, T), BF)


def route_body(partner, x, out):
    for r in range(16):
        out[r] = x[partner[r]]


def scratch(count):
    return [
        pltpu.VMEM((HEADS * T, F), BF),
        pltpu.VMEM((count, T, F), BF),
        pltpu.VMEM((count, HEADS * T, F), BF),
        pltpu.VMEM((count, 8, T), F32),
        pltpu.VMEM((count, 8, T), F32),
        pltpu.VMEM((4, T, 8), F32),
        pltpu.VMEM((T, F), F32),
        pltpu.VMEM((3, T, T), F32),
    ]


def sds(shape, dtype):
    return jax.ShapeDtypeStruct(shape, dtype)


def move(last, rows, p, h, jit, slots, consts):
    r0, r1, g = rows
    wqkv, wo, charge, falloff, headw, levels, heat = consts
    gx = lax.axis_size("gx")
    swap = [(0, 1), (1, 0)]
    fwd = [(i, i + 1) for i in range(gx - 1)]
    bwd = [(i + 1, i) for i in range(gx - 1)]
    gin = lax.ppermute(g, "gy", swap)
    up = lax.ppermute(r1, "gx", fwd)
    down = lax.ppermute(r0, "gx", bwd)
    macc, frow = call(
        own_body,
        "own",
        (sds((4 * T, F), F32), sds((16, T), F32)),
        [sm()] * 3 + [vm()] * 5,
        scratch(4),
    )(slots, falloff, headw, r0, r1, p, wqkv, charge)
    c0 = lax.ppermute(gin[1:2], "gx", fwd)
    c1 = lax.ppermute(gin[0:1], "gx", bwd)
    if last:
        outs = (sds((4 * T, F), BF), sds((12, T), F32), sds((12, T), F32))
    else:
        outs = sds((16, XR, F), BF)
    return call(
        lambda *refs: rest_body(last, *refs),
        "rest",
        outs,
        [sm()] * 5 + [vm()] * 15,
        scratch(8),
    )(
        slots, falloff, headw, levels, heat, r0, r1, p, h, jit, up, down, gin, c0, c1,
        macc, frow, wqkv, wo, charge,
    )


def per_device(
    descriptors, locations, jit1, jit2, slots, levels, heat, partner,
    gain, wqkv, wo, charge, falloff, headw,
):
    h0 = descriptors.reshape(4 * T, F)
    p0 = locations.reshape(12, T)
    jit1 = jit1.reshape(12, T)
    jit2 = jit2.reshape(12, T)
    slots = slots.reshape(4 * K)
    gain = gain.reshape(1, F)
    charge = jnp.broadcast_to(charge.reshape(1, F), (8, F))
    side = lax.axis_index("gy").reshape(1).astype(jnp.int32)
    consts = (wqkv, wo, charge, falloff, headw, levels, heat)
    row = sds((2, PR, F), BF)
    rows = call(
        first_body, "first", (row, row, row), [sm()] + [vm()] * 3, [pltpu.VMEM((4, 16, T), F32)]
    )(side, h0, p0, gain)
    x = move(False, rows, p0, h0, jit1, slots, consts)
    x = lax.all_to_all(x, "rep", split_axis=0, concat_axis=0, tiled=True)
    x = call(route_body, "route", sds((16, XR, F), BF), [sm(), vm()])(partner, x)
    x = lax.all_to_all(x, "rep", split_axis=0, concat_axis=0, tiled=True)
    r0, r1, g, h1, p1 = call(
        second_body,
        "second",
        (row, row, row, sds((4 * T, F), BF), sds((12, T), F32)),
        [sm()] + [vm()] * 2,
        [pltpu.VMEM((4, 16, T), F32)],
    )(side, x, gain)
    h2, p2, f2 = move(True, (r0, r1, g), p1, h1, jit2, slots, consts)
    return (
        h2.reshape(1, 2, 2, T, F),
        p2.reshape(1, 3, 2, 2, T),
        f2.reshape(1, 3, 2, 2, T),
    )


def solution(mesh):
    in_specs = (
        P("rep", "gx", "gy", None, None),
        P("rep", None, "gx", "gy", None),
        P("rep", None, "gx", "gy", None),
        P("rep", None, "gx", "gy", None),
        P("gx", "gy", None),
        P(),
        P("rep"),
        P(),
        P(),
        P(),
        P(),
        P(),
        P(),
        P(),
    )
    out_specs = (
        P("rep", "gx", "gy", None, None),
        P("rep", None, "gx", "gy", None),
        P("rep", None, "gx", "gy", None),
    )
    return jax.shard_map(
        per_device, mesh=mesh, in_specs=in_specs, out_specs=out_specs, check_vma=False
    )
```

```python
import math

import jax
import jax.numpy as jnp
from jax import lax
from jax.experimental import pallas as pl
from jax.experimental.pallas import tpu as pltpu
from jax.sharding import PartitionSpec as P

F = 128
HEADS = 8
HD = 16
T = 128
K = 6
PR = T + 16
XR = 40
NORM_EPS = 1e-05
DELTA = 0.1
JITTER = 0.05
MESSAGE_SCALE = 1.0 / 32.0
FORCE_SCALE = 1.0 / 16.0
LOG2E = 1.4426950408889634
ROWS = 64
WIDE = 3
STORED = (-1, 10, 4, 5, 10, 8, 0, 1, 8, 9, 2, 3, 9, 11, 6, 7, 11)
INTERPRET = False

BF = jnp.bfloat16
F32 = jnp.float32


def cos_half_coefs():
    return (
        0.9999999997799036,
        -1.2337005342697012,
        0.2536693224722507,
        -0.020862687547626383,
        0.000917723882055615,
        -2.3824535481836604e-05,
    )


def call(body, name, out_shape, in_specs, scratch=()):
    return pl.pallas_call(
        body,
        name=name,
        out_shape=out_shape,
        in_specs=in_specs,
        scratch_shapes=scratch,
        interpret=INTERPRET,
    )


def vm():
    return pl.BlockSpec(memory_space=pltpu.VMEM)


def sm():
    return pl.BlockSpec(memory_space=pltpu.SMEM)


def parts3(x):
    hi = x.astype(BF).astype(F32)
    rest = x - hi
    mid = rest.astype(BF).astype(F32)
    lo = rest - mid
    return hi, mid, lo


def norm_rows(h, gain):
    x = h.astype(F32)
    mean = jnp.mean(x, axis=-1, keepdims=True)
    xc = x - mean
    var = jnp.mean(xc * xc, axis=-1, keepdims=True)
    return (xc * lax.rsqrt(var + NORM_EPS) * gain).astype(BF)


def emit_rows(side, tiles, coords, r0, r1, g, cbuf):
    blocks = []
    for t in range(4):
        cbuf[t] = jnp.zeros((16, T), F32)
        for c in range(3):
            for k, part in enumerate(parts3(coords(c, t))):
                cbuf[t, c * 3 + k : c * 3 + k + 1, :] = part
        blocks.append(cbuf[t].astype(BF))
    for t in range(4):
        dst = r0 if t < 2 else r1
        dst[t % 2, 0:T, :] = tiles[t]
        dst[t % 2, T:PR, :] = blocks[t]
    for la in range(2):
        pick = side == 0
        g[la, 0:T, :] = jnp.where(pick, tiles[2 * la + 1], tiles[2 * la])
        g[la, T:PR, :] = jnp.where(pick, blocks[2 * la + 1], blocks[2 * la])


def first_body(side, h, p, gain, r0, r1, g, cbuf):
    tiles = [norm_rows(h[0, t // 2, t % 2], gain[...]) for t in range(4)]
    emit_rows(side[0], tiles, lambda c, t: own_rows(p, t)[c], r0, r1, g, cbuf)


def second_body(side, x, gain, r0, r1, g, h, p, cbuf):
    tiles = []
    for t in range(4):
        for c in range(3):
            blk = x[4 * t + c, 32:40, :].astype(F32)
            p[0, c, t // 2, t % 2 : t % 2 + 1, :] = blk[0:1] + blk[1:2] + blk[2:3]
        for q in range(4):
            h[t * T + q * 32 : t * T + (q + 1) * 32, :] = x[4 * t + q, 0:32, :]
        tiles.append(norm_rows(h[t * T : (t + 1) * T, :], gain[...]))
    emit_rows(side[0], tiles, lambda c, t: own_rows(p, t)[c], r0, r1, g, cbuf)


def head_mask(e, shape):
    lane = lax.broadcasted_iota(jnp.int32, shape, 1)
    return (lane & (F - 1)) // HD == e


def origin(p):
    return [p[0, c, 0, 0:1, 0:1] for c in range(3)]


def project_kv(tile, n, rows, center, wkv, charge, kbuf, vbuf, jbuf):
    kv = jnp.dot(tile, wkv, preferred_element_type=F32)
    k = kv[:, :F].astype(BF)
    kbuf[n] = k
    probe = lax.dot_general(charge, k, (((1,), (1,)), ((), ())), preferred_element_type=F32)[0:1]
    terms = [probe] + [probe * (rows[c] - center[c]) for c in range(3)]
    stack = [part for term in terms for part in parts3(term)] + [jnp.zeros((4, T), F32)]
    force = jnp.concatenate(stack, axis=0)
    force = jnp.concatenate([force] * HEADS, axis=0).T
    both = jnp.concatenate([kv[:, F:], force], axis=1).astype(BF)
    zero = jnp.zeros_like(both)
    for e in range(HEADS):
        vbuf[n, e * T : (e + 1) * T, :] = jnp.where(head_mask(e, both.shape), both, zero)
    jbuf[n] = jnp.concatenate(list(rows) + [jnp.zeros((5, T), F32)], axis=0)


def project_q(tile, m, wq, qbuf):
    q = jnp.dot(tile, wq, preferred_element_type=F32).astype(BF)
    q = q * jnp.asarray(0.125, BF)
    zero = jnp.zeros_like(q)
    for e in range(HEADS):
        qbuf[m, e * T : (e + 1) * T, :] = jnp.where(head_mask(e, q.shape), q, zero)


def geometry(mine, near, limit, i):
    mine = mine[i * ROWS : (i + 1) * ROWS, :]
    d = [mine[:, c : c + 1] - near[c : c + 1, :] for c in range(3)]
    r2 = d[0] * d[0] + d[1] * d[1] + d[2] * d[2]
    coefs = cos_half_coefs()
    poly = r2 * coefs[-1] + coefs[-2]
    for cf in coefs[-3::-1]:
        poly = poly * r2 + cf
    return r2, jnp.where(r2 < limit, poly * poly, 0.0).astype(BF)


def pair_terms(m, n, limit, decays, qbuf, kbuf, vbuf, jbuf, ibuf, macc):
    near = jbuf[n]
    mine = ibuf[m]
    k = kbuf[n]
    parts = [geometry(mine, near, limit, i) for i in range(T // ROWS)]
    cut = jnp.concatenate([part[1] for part in parts], axis=0)
    ws = []
    for e2 in range(HEADS // 2):
        half = lax.dot_general(
            qbuf[m, e2 * 2 * T : (e2 + 1) * 2 * T, :],
            k,
            (((1,), (1,)), ((), ())),
            preferred_element_type=F32,
        ).astype(BF)
        for s in range(2):
            e = e2 * 2 + s
            u = half[s * T : (s + 1) * T, :]
            power = jnp.concatenate([(part[0] * decays[e]).astype(BF) for part in parts], axis=0)
            ws.append((u + u * jnp.tanh(u)) * (jnp.exp2(power) * cut))
    macc[m] += jnp.dot(jnp.concatenate(ws, axis=1), vbuf[n], preferred_element_type=F32)


def visit(slots, table, falloff, lo, hi, todo, qbuf, kbuf, vbuf, jbuf, ibuf, macc):
    count = jnp.int32(0)
    for t in range(4):
        for s in range(K):
            n = table[slots[t // 2, t % 2, s] + 1]
            todo[count] = (n - lo) * 4 + t
            count = count + jnp.where((n >= lo) & (n < hi), 1, 0)
    todo[count] = 0
    decays = [falloff[e] * (-LOG2E) for e in range(HEADS)]

    def step(i, carry):
        for s in range(WIDE):
            at = i * WIDE + s
            code = todo[at]
            limit = jnp.where(at < count, 1.0, 0.0)
            n = code // 4
            pair_terms(
                code - n * 4, n, limit, decays, qbuf, kbuf, vbuf, jbuf, ibuf, macc
            )
        return carry

    lax.fori_loop(0, (count + WIDE - 1) // WIDE, step, 0)


def own_rows(p, t):
    return [p[0, c, t // 2, t % 2 : t % 2 + 1, :] for c in range(3)]


def own_columns(p, ibuf, t):
    ibuf[t] = jnp.concatenate(own_rows(p, t) + [jnp.zeros((5, T), F32)], axis=0).T


def own_body(
    slots, table, falloff, r0, r1, p, wqkv, charge, macc, todo, qbuf, kbuf, vbuf, jbuf, ibuf
):
    center = origin(p)
    for t in range(4):
        tile = (r0 if t < 2 else r1)[t % 2, 0:T, :]
        project_kv(
            tile, t, own_rows(p, t), center, wqkv[:, F:], charge_rows(charge), kbuf, vbuf, jbuf
        )
        project_q(tile, t, wqkv[:, :F], qbuf)
        own_columns(p, ibuf, t)
        macc[t] = jnp.zeros((T, 2 * F), F32)
    visit(slots, table, falloff, 0, 4, todo, qbuf, kbuf, vbuf, jbuf, ibuf, macc)


def charge_rows(charge):
    return jnp.broadcast_to(charge[...].astype(F32), (16, F)).astype(BF)


def rest_body(
    last,
    slots, table, falloff, headw, levels, heat, r0, r1, p, h, jit, up, down, gin, c0, c1,
    macc_in, wqkv, wo, charge,
    *refs,
):
    if last:
        hout, pout, fout = refs[:3]
        refs = refs[3:]
    else:
        xout = refs[0]
        refs = refs[1:]
    todo, qbuf, kbuf, vbuf, jbuf, ibuf, macc = refs
    center = origin(p)
    halo = [(up, 0), (up, 1), (down, 0), (down, 1), (gin, 0), (gin, 1), (c0, 0), (c1, 0)]
    for i, (src, a) in enumerate(halo):
        blk = src[a, T:PR, :].astype(F32)
        rows = [
            blk[3 * c : 3 * c + 1] + blk[3 * c + 1 : 3 * c + 2] + blk[3 * c + 2 : 3 * c + 3]
            for c in range(3)
        ]
        project_kv(
            src[a, 0:T, :], i, rows, center, wqkv[:, F:], charge_rows(charge), kbuf, vbuf, jbuf
        )
    scale = JITTER * jnp.sqrt(jnp.full((1, T), levels[heat[0]], F32))
    for t in range(4):
        own_columns(p, ibuf, t)
        project_q((r0 if t < 2 else r1)[t % 2, 0:T, :], t, wqkv[:, :F], qbuf)
        macc[t] = macc_in[t]
    visit(slots, table, falloff, 4, 12, todo, qbuf, kbuf, vbuf, jbuf, ibuf, macc)
    for t in range(4):
        a, b = t // 2, t % 2
        message = (macc[t, :, :F] * MESSAGE_SCALE).astype(BF)
        mixed = jnp.dot(message, wo[...], preferred_element_type=F32)
        old = h[0, a, b] if len(h.shape) == 5 else h[t * T : (t + 1) * T, :]
        updated = (old.astype(F32) + mixed).astype(BF)
        if last:
            hout[0, a, b] = updated
        else:
            for q in range(4):
                xout[4 * t + q, 0:32, :] = updated[q * 32 : (q + 1) * 32, :]
        terms = macc[t, :, F:].T
        total = terms[0:HD, :] * headw[0]
        for e in range(1, HEADS):
            total = total + terms[e * HD : (e + 1) * HD, :] * headw[e]
        sums = [total[3 * c : 3 * c + 1] + total[3 * c + 1 : 3 * c + 2] + total[3 * c + 2 : 3 * c + 3] for c in range(4)]
        for c, row in enumerate(own_rows(p, t)):
            force = ((row - center[c]) * sums[0] - sums[c + 1]) * FORCE_SCALE
            moved = row + DELTA * force + scale * jit[0, c, a, b : b + 1, :]
            if last:
                pout[0, c, a, b : b + 1, :] = moved
                fout[0, c, a, b : b + 1, :] = force
            else:
                xout[4 * t + c, 32:40, :] = jnp.concatenate(
                    list(parts3(moved)) + [jnp.zeros((5, T), F32)], axis=0
                ).astype(BF)
        if not last:
            xout[4 * t + 3, 32:40, :] = jnp.zeros((8, T), BF)


def route_body(partner, x, out):
    for r in range(16):
        out[r] = x[partner[r]]


def scratch(count):
    return [
        pltpu.SMEM((4 * K + WIDE,), jnp.int32),
        pltpu.VMEM((4, HEADS * T, F), BF),
        pltpu.VMEM((count, T, F), BF),
        pltpu.VMEM((count, HEADS * T, 2 * F), BF),
        pltpu.VMEM((count, 8, T), F32),
        pltpu.VMEM((4, T, 8), F32),
    ]


def sds(shape, dtype):
    return jax.ShapeDtypeStruct(shape, dtype)


HSHAPE = (1, 2, 2, T, F)
PSHAPE = (1, 3, 2, 2, T)


def move(last, rows, p, h, jit, slots, consts):
    r0, r1, g = rows
    table = jnp.asarray(STORED, jnp.int32)
    wqkv, wo, charge, falloff, headw, levels, heat = consts
    gx = lax.axis_size("gx")
    swap = [(0, 1), (1, 0)]
    fwd = [(i, i + 1) for i in range(gx - 1)]
    bwd = [(i + 1, i) for i in range(gx - 1)]
    gin = lax.ppermute(g, "gy", swap)
    up = lax.ppermute(r1, "gx", fwd)
    down = lax.ppermute(r0, "gx", bwd)
    macc = call(
        own_body,
        "own",
        sds((4, T, 2 * F), F32),
        [sm()] * 3 + [vm()] * 5,
        scratch(4),
    )(slots, table, falloff, r0, r1, p, wqkv, charge)
    gin, macc = lax.optimization_barrier((gin, macc))
    c0 = lax.ppermute(gin[1:2], "gx", fwd)
    c1 = lax.ppermute(gin[0:1], "gx", bwd)
    if last:
        outs = (sds(HSHAPE, BF), sds(PSHAPE, F32), sds(PSHAPE, F32))
    else:
        outs = sds((16, XR, F), BF)
    return call(
        lambda *refs: rest_body(last, *refs),
        "rest",
        outs,
        [sm()] * 6 + [vm()] * 14,
        scratch(8) + [pltpu.VMEM((4, T, 2 * F), F32)],
    )(
        slots, table, falloff, headw, levels, heat, r0, r1, p, h, jit, up, down, gin, c0, c1,
        macc, wqkv, wo, charge,
    )


def per_device(
    descriptors, locations, jit1, jit2, slots, levels, heat, partner,
    gain, wqkv, wo, charge, falloff, headw,
):
    gain = gain.reshape(1, F)
    charge = charge.reshape(1, F)
    side = lax.axis_index("gy").reshape(1).astype(jnp.int32)
    consts = (wqkv, wo, charge, falloff, headw, levels, heat)
    row = sds((2, PR, F), BF)
    rows = call(
        first_body, "first", (row, row, row), [sm()] + [vm()] * 3, [pltpu.VMEM((4, 16, T), F32)]
    )(side, descriptors, locations, gain)
    x = move(False, rows, locations, descriptors, jit1, slots, consts)
    x = lax.all_to_all(x, "rep", split_axis=0, concat_axis=0, tiled=True)
    x = call(route_body, "route", sds((16, XR, F), BF), [sm(), vm()])(partner, x)
    x = lax.all_to_all(x, "rep", split_axis=0, concat_axis=0, tiled=True)
    r0, r1, g, h1, p1 = call(
        second_body,
        "second",
        (row, row, row, sds((4 * T, F), BF), sds(PSHAPE, F32)),
        [sm()] + [vm()] * 2,
        [pltpu.VMEM((4, 16, T), F32)],
    )(side, x, gain)
    return move(True, (r0, r1, g), p1, h1, jit2, slots, consts)


def solution(mesh):
    in_specs = (
        P("rep", "gx", "gy", None, None),
        P("rep", None, "gx", "gy", None),
        P("rep", None, "gx", "gy", None),
        P("rep", None, "gx", "gy", None),
        P("gx", "gy", None),
        P(),
        P("rep"),
        P(),
        P(),
        P(),
        P(),
        P(),
        P(),
        P(),
    )
    out_specs = (
        P("rep", "gx", "gy", None, None),
        P("rep", None, "gx", "gy", None),
        P("rep", None, "gx", "gy", None),
    )
    return jax.shard_map(
        per_device, mesh=mesh, in_specs=in_specs, out_specs=out_specs, check_vma=False
    )
```

```python
import math

import jax
import jax.numpy as jnp
from jax import lax
from jax.experimental import pallas as pl
from jax.experimental.pallas import tpu as pltpu
from jax.sharding import PartitionSpec as P

F = 128
HEADS = 8
HD = 16
T = 128
K = 6
PR = T + 16
XR = 40
NORM_EPS = 1e-05
DELTA = 0.1
JITTER = 0.05
MESSAGE_SCALE = 1.0 / 32.0
FORCE_SCALE = 1.0 / 16.0
LOG2E = 1.4426950408889634
ROWS = 64
SIDE = 4
WIDE = 3
STORED = (-1, 10, 4, 5, 10, 8, 0, 1, 8, 9, 2, 3, 9, 11, 6, 7, 11)
INTERPRET = False

BF = jnp.bfloat16
F32 = jnp.float32


def cos_half_coefs():
    return (
        0.9999999997799036,
        -1.2337005342697012,
        0.2536693224722507,
        -0.020862687547626383,
        0.000917723882055615,
        -2.3824535481836604e-05,
    )


def call(body, name, out_shape, in_specs, scratch=()):
    many = isinstance(out_shape, tuple)
    out_specs = (vm(),) * len(out_shape) if many else vm()
    return pl.pallas_call(
        body,
        name=name,
        out_shape=out_shape,
        in_specs=in_specs,
        out_specs=out_specs,
        scratch_shapes=scratch,
        interpret=INTERPRET,
    )


def near(x):
    return x if INTERPRET else pltpu.with_memory_space_constraint(x, pltpu.VMEM)


def sds(shape, dtype):
    return jax.ShapeDtypeStruct(shape, dtype)


def vout(shape, dtype):
    return sds(shape, dtype) if INTERPRET else pltpu.VMEM(shape, dtype)


def vm():
    return pl.BlockSpec(memory_space=pltpu.VMEM)


def sm():
    return pl.BlockSpec(memory_space=pltpu.SMEM)


def parts3(x):
    hi = x.astype(BF).astype(F32)
    rest = x - hi
    mid = rest.astype(BF).astype(F32)
    lo = rest - mid
    return hi, mid, lo


def norm_rows(h, gain):
    x = h.astype(F32)
    mean = jnp.mean(x, axis=-1, keepdims=True)
    xc = x - mean
    var = jnp.mean(xc * xc, axis=-1, keepdims=True)
    return (xc * lax.rsqrt(var + NORM_EPS) * gain).astype(BF)


def emit_rows(side, tiles, coords, r0, r1, g, cbuf):
    blocks = []
    for t in range(4):
        cbuf[t] = jnp.zeros((16, T), F32)
        for c in range(3):
            for k, part in enumerate(parts3(coords(c, t))):
                cbuf[t, c * 3 + k : c * 3 + k + 1, :] = part
        blocks.append(cbuf[t].astype(BF))
    for t in range(4):
        dst = r0 if t < 2 else r1
        dst[t % 2, 0:T, :] = tiles[t]
        dst[t % 2, T:PR, :] = blocks[t]
    for la in range(2):
        pick = side == 0
        g[la, 0:T, :] = jnp.where(pick, tiles[2 * la + 1], tiles[2 * la])
        g[la, T:PR, :] = jnp.where(pick, blocks[2 * la + 1], blocks[2 * la])


def first_body(side, h, p, gain, r0, r1, g, cbuf):
    tiles = [norm_rows(h[0, t // 2, t % 2], gain[...]) for t in range(4)]
    emit_rows(side[0], tiles, lambda c, t: own_rows(p, t)[c], r0, r1, g, cbuf)


def second_body(side, rep, x0, x1, x2, x3, gain, r0, r1, g, h, p, cbuf):
    for k, x in enumerate((x0, x1, x2, x3)):
        t = (rep[0] // SIDE) ^ k
        for c in range(3):
            blk = x[c, 32:40, :].astype(F32)
            cbuf[0, c : c + 1, :] = blk[0:1] + blk[1:2] + blk[2:3]
            p[0, c, t // 2, pl.ds(t % 2, 1), :] = cbuf[0, c : c + 1, :]
        for q in range(SIDE):
            h[t, q * 32 : (q + 1) * 32, :] = x[q, 0:32, :]
    tiles = [norm_rows(h[t], gain[...]) for t in range(4)]
    emit_rows(side[0], tiles, lambda c, t: own_rows(p, t)[c], r0, r1, g, cbuf)


def head_mask(e, shape):
    lane = lax.broadcasted_iota(jnp.int32, shape, 1)
    return (lane & (F - 1)) // HD == e


def origin(p):
    return [p[0, c, 0, 0:1, 0:1] for c in range(3)]


def project_kv(tile, n, rows, center, wkv, charge, kbuf, vbuf, jbuf):
    kv = jnp.dot(tile, wkv, preferred_element_type=F32)
    k = kv[:, :F].astype(BF)
    kbuf[n] = k
    probe = lax.dot_general(charge, k, (((1,), (1,)), ((), ())), preferred_element_type=F32)[0:1]
    terms = [probe] + [probe * (rows[c] - center[c]) for c in range(3)]
    stack = [part for term in terms for part in parts3(term)] + [jnp.zeros((4, T), F32)]
    force = jnp.concatenate(stack, axis=0)
    force = jnp.concatenate([force] * HEADS, axis=0).T
    both = jnp.concatenate([kv[:, F:], force], axis=1).astype(BF)
    zero = jnp.zeros_like(both)
    for e in range(HEADS):
        vbuf[n, e * T : (e + 1) * T, :] = jnp.where(head_mask(e, both.shape), both, zero)
    jbuf[n] = jnp.concatenate(list(rows) + [jnp.zeros((5, T), F32)], axis=0)


def project_q(tile, m, wq, qbuf):
    q = jnp.dot(tile, wq, preferred_element_type=F32).astype(BF)
    q = q * jnp.asarray(0.125, BF)
    zero = jnp.zeros_like(q)
    for e in range(HEADS):
        qbuf[m, e * T : (e + 1) * T, :] = jnp.where(head_mask(e, q.shape), q, zero)


def geometry(mine, near, limit, i):
    mine = mine[i * ROWS : (i + 1) * ROWS, :]
    d = [mine[:, c : c + 1] - near[c : c + 1, :] for c in range(3)]
    r2 = d[0] * d[0] + d[1] * d[1] + d[2] * d[2]
    coefs = cos_half_coefs()
    poly = r2 * coefs[-1] + coefs[-2]
    for cf in coefs[-3::-1]:
        poly = poly * r2 + cf
    return r2, jnp.where(r2 < limit, poly * poly, 0.0).astype(BF)


def pair_terms(m, n, limit, decays, qbuf, kbuf, vbuf, jbuf, ibuf, macc):
    near = jbuf[n]
    mine = ibuf[m]
    k = kbuf[n]
    parts = [geometry(mine, near, limit, i) for i in range(T // ROWS)]
    cut = jnp.concatenate([part[1] for part in parts], axis=0)
    ws = []
    for e2 in range(HEADS // 2):
        half = lax.dot_general(
            qbuf[m, e2 * 2 * T : (e2 + 1) * 2 * T, :],
            k,
            (((1,), (1,)), ((), ())),
            preferred_element_type=F32,
        ).astype(BF)
        for s in range(2):
            e = e2 * 2 + s
            u = half[s * T : (s + 1) * T, :]
            power = jnp.concatenate([(part[0] * decays[e]).astype(BF) for part in parts], axis=0)
            ws.append((u + u * jnp.tanh(u)) * (jnp.exp2(power) * cut))
    macc[m] += jnp.dot(jnp.concatenate(ws, axis=1), vbuf[n], preferred_element_type=F32)


def visit(slots, table, falloff, lo, hi, todo, qbuf, kbuf, vbuf, jbuf, ibuf, macc):
    count = jnp.int32(0)
    for t in range(4):
        for s in range(K):
            n = table[slots[t // 2, t % 2, s] + 1]
            todo[count] = (n - lo) * 4 + t
            count = count + jnp.where((n >= lo) & (n < hi), 1, 0)
    todo[count] = 0
    decays = [falloff[e] * (-LOG2E) for e in range(HEADS)]

    def step(i, carry):
        for s in range(WIDE):
            at = i * WIDE + s
            code = todo[at]
            limit = jnp.where(at < count, 1.0, 0.0)
            n = code // 4
            pair_terms(
                code - n * 4, n, limit, decays, qbuf, kbuf, vbuf, jbuf, ibuf, macc
            )
        return carry

    lax.fori_loop(0, (count + WIDE - 1) // WIDE, step, 0)


def own_rows(p, t):
    return [p[0, c, t // 2, t % 2 : t % 2 + 1, :] for c in range(3)]


def own_columns(p, ibuf, t):
    ibuf[t] = jnp.concatenate(own_rows(p, t) + [jnp.zeros((5, T), F32)], axis=0).T


def own_body(
    slots, table, falloff, r0, r1, p, wqkv, charge, macc, todo, qbuf, kbuf, vbuf, jbuf, ibuf
):
    center = origin(p)
    for t in range(4):
        tile = (r0 if t < 2 else r1)[t % 2, 0:T, :]
        project_kv(
            tile, t, own_rows(p, t), center, wqkv[:, F:], charge_rows(charge), kbuf, vbuf, jbuf
        )
        project_q(tile, t, wqkv[:, :F], qbuf)
        own_columns(p, ibuf, t)
        macc[t] = jnp.zeros((T, 2 * F), F32)
    visit(slots, table, falloff, 0, 4, todo, qbuf, kbuf, vbuf, jbuf, ibuf, macc)


def charge_rows(charge):
    return jnp.broadcast_to(charge[...].astype(F32), (16, F)).astype(BF)


def rest_body(
    last,
    slots, table, falloff, headw, levels, heat, rep, r0, r1, p, h, jit, up, down, gin, c0, c1,
    macc_in, wqkv, wo, charge,
    *refs,
):
    if last:
        hout, pout, fout = refs[:3]
        refs = refs[3:]
    else:
        sends = refs[:SIDE]
        xout = refs[-1]
        refs = refs[SIDE:-1]
    todo, qbuf, kbuf, vbuf, jbuf, ibuf, macc = refs
    center = origin(p)
    halo = [(up, 0), (up, 1), (down, 0), (down, 1), (gin, 0), (gin, 1), (c0, 0), (c1, 0)]
    for i, (src, a) in enumerate(halo):
        blk = src[a, T:PR, :].astype(F32)
        rows = [
            blk[3 * c : 3 * c + 1] + blk[3 * c + 1 : 3 * c + 2] + blk[3 * c + 2 : 3 * c + 3]
            for c in range(3)
        ]
        project_kv(
            src[a, 0:T, :], i, rows, center, wqkv[:, F:], charge_rows(charge), kbuf, vbuf, jbuf
        )
    scale = JITTER * jnp.sqrt(jnp.full((1, T), levels[heat[0]], F32))
    for t in range(4):
        own_columns(p, ibuf, t)
        project_q((r0 if t < 2 else r1)[t % 2, 0:T, :], t, wqkv[:, :F], qbuf)
        macc[t] = macc_in[t]
    visit(slots, table, falloff, 4, 12, todo, qbuf, kbuf, vbuf, jbuf, ibuf, macc)
    for t in range(4):
        a, b = t // 2, t % 2
        message = (macc[t, :, :F] * MESSAGE_SCALE).astype(BF)
        mixed = jnp.dot(message, wo[...], preferred_element_type=F32)
        old = h[0, a, b] if len(h.shape) == 5 else h[t]
        updated = (old.astype(F32) + mixed).astype(BF)
        if last:
            hout[0, a, b] = updated
        else:
            for q in range(4):
                xout[4 * t + q, 0:32, :] = updated[q * 32 : (q + 1) * 32, :]
        terms = macc[t, :, F:].T
        total = terms[0:HD, :] * headw[0]
        for e in range(1, HEADS):
            total = total + terms[e * HD : (e + 1) * HD, :] * headw[e]
        sums = [total[3 * c : 3 * c + 1] + total[3 * c + 1 : 3 * c + 2] + total[3 * c + 2 : 3 * c + 3] for c in range(4)]
        for c, row in enumerate(own_rows(p, t)):
            force = ((row - center[c]) * sums[0] - sums[c + 1]) * FORCE_SCALE
            moved = row + DELTA * force + scale * jit[0, c, a, b : b + 1, :]
            if last:
                pout[0, c, a, b : b + 1, :] = moved
                fout[0, c, a, b : b + 1, :] = force
            else:
                xout[4 * t + c, 32:40, :] = jnp.concatenate(
                    list(parts3(moved)) + [jnp.zeros((5, T), F32)], axis=0
                ).astype(BF)
        if not last:
            xout[4 * t + 3, 32:40, :] = jnp.zeros((8, T), BF)
    if not last:
        mine = rep[0] // SIDE
        for k in range(SIDE):
            for q in range(SIDE):
                sends[k][q] = xout[(mine ^ k) * SIDE + q]


def spread_body(rep, x0, x1, x2, x3, y0, y1, y2, y3):
    z, y = rep[0] // SIDE, rep[0] % SIDE
    for j, out in enumerate((y0, y1, y2, y3)):
        for k, x in enumerate((x0, x1, x2, x3)):
            out[z ^ k] = x[y ^ j]


def route_body(rep, partner, x0, x1, x2, x3, y0, y1, y2, y3, buf):
    y = rep[0] % SIDE
    for k, x in enumerate((x0, x1, x2, x3)):
        for row in range(SIDE):
            buf[row * SIDE + (y ^ k)] = x[row]
    for k, out in enumerate((y0, y1, y2, y3)):
        for row in range(SIDE):
            out[row] = buf[partner[row * SIDE + (y ^ k)]]


def gather_body(rep, x0, x1, x2, x3, y0, y1, y2, y3):
    z, y = rep[0] // SIDE, rep[0] % SIDE
    for j, out in enumerate((y0, y1, y2, y3)):
        for k, x in enumerate((x0, x1, x2, x3)):
            out[y ^ k] = x[z ^ j]


def pieces():
    return (vout((SIDE, XR, F), BF),) * SIDE


def stage(blocks, along_rows):
    count = lax.axis_size("rep")
    out = [near(blocks[0])]
    for k in range(1, SIDE):
        flip = k * SIDE if along_rows else k
        moved = lax.ppermute(blocks[k], "rep", [(r, r ^ flip) for r in range(count)])
        out.append(near(moved))
    return out


def scratch(count):
    return [
        pltpu.SMEM((4 * K + WIDE,), jnp.int32),
        pltpu.VMEM((4, HEADS * T, F), BF),
        pltpu.VMEM((count, T, F), BF),
        pltpu.VMEM((count, HEADS * T, 2 * F), BF),
        pltpu.VMEM((count, 8, T), F32),
        pltpu.VMEM((4, T, 8), F32),
    ]


HSHAPE = (1, 2, 2, T, F)
PSHAPE = (1, 3, 2, 2, T)


def move(last, rows, p, h, jit, slots, rep, consts):
    r0, r1, g = rows
    table = jnp.asarray(STORED, jnp.int32)
    wqkv, wo, charge, falloff, headw, levels, heat = consts
    gx = lax.axis_size("gx")
    swap = [(0, 1), (1, 0)]
    fwd = [(i, (i + 1) % gx) for i in range(gx)]
    bwd = [((i + 1) % gx, i) for i in range(gx)]
    gin = lax.ppermute(g, "gy", swap)
    up = near(lax.ppermute(r1, "gx", fwd))
    down = near(lax.ppermute(r0, "gx", bwd))
    macc = call(
        own_body,
        "own",
        vout((4, T, 2 * F), F32),
        [sm()] * 3 + [vm()] * 5,
        scratch(4),
    )(slots, table, falloff, near(r0), near(r1), p, wqkv, charge)
    gin, macc = lax.optimization_barrier((gin, macc))
    c0 = near(lax.ppermute(gin[1:2], "gx", fwd))
    c1 = near(lax.ppermute(gin[0:1], "gx", bwd))
    if last:
        outs = (sds(HSHAPE, BF), sds(PSHAPE, F32), sds(PSHAPE, F32))
        more = []
    else:
        outs = pieces()
        more = [pltpu.VMEM((16, XR, F), BF)]
    return call(
        lambda *refs: rest_body(last, *refs),
        "rest",
        outs,
        [sm()] * 7 + [vm()] * 14,
        scratch(8) + [pltpu.VMEM((4, T, 2 * F), F32)] + more,
    )(
        slots, table, falloff, headw, levels, heat, rep, near(r0), near(r1), p, h, jit, up, down,
        near(gin), c0, c1, near(macc), wqkv, wo, charge,
    )


def per_device(
    descriptors, locations, jit1, jit2, slots, levels, heat, partner,
    gain, wqkv, wo, charge, falloff, headw,
):
    gain = near(gain.reshape(1, F))
    charge = near(charge.reshape(1, F))
    wqkv = near(wqkv)
    wo = near(wo)
    side = lax.axis_index("gy").reshape(1).astype(jnp.int32)
    rep = lax.axis_index("rep").reshape(1).astype(jnp.int32)
    consts = (wqkv, wo, charge, falloff, headw, levels, heat)
    row = vout((2, PR, F), BF)
    rows = call(
        first_body, "first", (row, row, row), [sm()] + [vm()] * 3, [pltpu.VMEM((4, 16, T), F32)]
    )(side, descriptors, locations, gain)
    x = move(False, rows, locations, descriptors, near(jit1), slots, rep, consts)
    x = stage(x, True)
    x = call(spread_body, "spread", pieces(), [sm()] + [vm()] * SIDE)(rep, *x)
    x = stage(x, False)
    x = call(
        route_body,
        "route",
        pieces(),
        [sm()] * 2 + [vm()] * SIDE,
        [pltpu.VMEM((16, XR, F), BF)],
    )(rep, partner, *x)
    x = stage(x, False)
    x = call(gather_body, "gather", pieces(), [sm()] + [vm()] * SIDE)(rep, *x)
    x = stage(x, True)
    r0, r1, g, h1, p1 = call(
        second_body,
        "second",
        (row, row, row, vout((4, T, F), BF), vout(PSHAPE, F32)),
        [sm()] * 2 + [vm()] * 5,
        [pltpu.VMEM((4, 16, T), F32)],
    )(side, rep, *x, gain)
    return move(True, (r0, r1, g), near(p1), near(h1), near(jit2), slots, rep, consts)


def solution(mesh):
    in_specs = (
        P("rep", "gx", "gy", None, None),
        P("rep", None, "gx", "gy", None),
        P("rep", None, "gx", "gy", None),
        P("rep", None, "gx", "gy", None),
        P("gx", "gy", None),
        P(),
        P("rep"),
        P(),
        P(),
        P(),
        P(),
        P(),
        P(),
        P(),
    )
    out_specs = (
        P("rep", "gx", "gy", None, None),
        P("rep", None, "gx", "gy", None),
        P("rep", None, "gx", "gy", None),
    )
    return jax.shard_map(
        per_device, mesh=mesh, in_specs=in_specs, out_specs=out_specs, check_vma=False
    )
```

```python
import math

import jax
import jax.numpy as jnp
from jax import lax
from jax.experimental import pallas as pl
from jax.experimental.pallas import tpu as pltpu
from jax.sharding import PartitionSpec as P

F = 128
HEADS = 8
HD = 16
T = 128
K = 6
PR = T + 16
XR = 40
NORM_EPS = 1e-05
DELTA = 0.1
JITTER = 0.05
MESSAGE_SCALE = 1.0 / 32.0
FORCE_SCALE = 1.0 / 16.0
LOG2E = 1.4426950408889634
ROWS = 64
WIDE = 3
STORED = (-1, 10, 4, 5, 10, 8, 0, 1, 8, 9, 2, 3, 9, 11, 6, 7, 11)
INTERPRET = False

BF = jnp.bfloat16
F32 = jnp.float32


def cos_half_coefs():
    return (
        0.9999999997799036,
        -1.2337005342697012,
        0.2536693224722507,
        -0.020862687547626383,
        0.000917723882055615,
        -2.3824535481836604e-05,
    )


def call(body, name, out_shape, in_specs, scratch=()):
    many = isinstance(out_shape, tuple)
    out_specs = (vm(),) * len(out_shape) if many else vm()
    return pl.pallas_call(
        body,
        name=name,
        out_shape=out_shape,
        in_specs=in_specs,
        out_specs=out_specs,
        scratch_shapes=scratch,
        compiler_params=pltpu.CompilerParams(vmem_limit_bytes=20 * 1024 * 1024),
        interpret=INTERPRET,
    )


def near(x):
    return x if INTERPRET else pltpu.with_memory_space_constraint(x, pltpu.VMEM)


def sds(shape, dtype):
    return jax.ShapeDtypeStruct(shape, dtype)


def vout(shape, dtype):
    return sds(shape, dtype) if INTERPRET else pltpu.VMEM(shape, dtype)


def vm():
    return pl.BlockSpec(memory_space=pltpu.VMEM)


def sm():
    return pl.BlockSpec(memory_space=pltpu.SMEM)


def parts3(x):
    hi = x.astype(BF).astype(F32)
    rest = x - hi
    mid = rest.astype(BF).astype(F32)
    lo = rest - mid
    return hi, mid, lo


def norm_rows(h, gain):
    x = h.astype(F32)
    mean = jnp.mean(x, axis=-1, keepdims=True)
    xc = x - mean
    var = jnp.mean(xc * xc, axis=-1, keepdims=True)
    return (xc * lax.rsqrt(var + NORM_EPS) * gain).astype(BF)


def emit_rows(side, tiles, coords, r0, r1, g, cbuf):
    blocks = []
    for t in range(4):
        cbuf[t] = jnp.zeros((16, T), F32)
        for c in range(3):
            for k, part in enumerate(parts3(coords(c, t))):
                cbuf[t, c * 3 + k : c * 3 + k + 1, :] = part
        blocks.append(cbuf[t].astype(BF))
    for t in range(4):
        dst = r0 if t < 2 else r1
        dst[t % 2, 0:T, :] = tiles[t]
        dst[t % 2, T:PR, :] = blocks[t]
    for la in range(2):
        pick = side == 0
        g[la, 0:T, :] = jnp.where(pick, tiles[2 * la + 1], tiles[2 * la])
        g[la, T:PR, :] = jnp.where(pick, blocks[2 * la + 1], blocks[2 * la])


def first_body(side, h, p, gain, r0, r1, g, cbuf):
    tiles = [norm_rows(h[0, t // 2, t % 2], gain[...]) for t in range(4)]
    emit_rows(side[0], tiles, lambda c, t: own_rows(p, t)[c], r0, r1, g, cbuf)


def second_body(side, x, gain, r0, r1, g, h, p, cbuf):
    for t in range(4):
        for c in range(3):
            blk = x[4 * t + c, 32:40, :].astype(F32)
            p[0, c, t // 2, t % 2 : t % 2 + 1, :] = blk[0:1] + blk[1:2] + blk[2:3]
        for q in range(4):
            h[t, q * 32 : (q + 1) * 32, :] = x[4 * t + q, 0:32, :]
    tiles = [norm_rows(h[t], gain[...]) for t in range(4)]
    emit_rows(side[0], tiles, lambda c, t: own_rows(p, t)[c], r0, r1, g, cbuf)


def head_mask(e, shape):
    lane = lax.broadcasted_iota(jnp.int32, shape, 1)
    return (lane & (F - 1)) // HD == e


def origin(p):
    return [p[0, c, 0, 0:1, 0:1] for c in range(3)]


def project_kv(tile, n, rows, center, wkv, charge, kbuf, vbuf, jbuf):
    kv = jnp.dot(tile, wkv, preferred_element_type=F32)
    k = kv[:, :F].astype(BF)
    kbuf[n] = k
    probe = lax.dot_general(charge, k, (((1,), (1,)), ((), ())), preferred_element_type=F32)[0:1]
    terms = [probe] + [probe * (rows[c] - center[c]) for c in range(3)]
    stack = [part for term in terms for part in parts3(term)] + [jnp.zeros((4, T), F32)]
    force = jnp.concatenate(stack, axis=0)
    force = jnp.concatenate([force] * HEADS, axis=0).T
    both = jnp.concatenate([kv[:, F:], force], axis=1).astype(BF)
    zero = jnp.zeros_like(both)
    for e in range(HEADS):
        vbuf[n, e * T : (e + 1) * T, :] = jnp.where(head_mask(e, both.shape), both, zero)
    jbuf[n] = jnp.concatenate(list(rows) + [jnp.zeros((5, T), F32)], axis=0)


def project_q(tile, m, wq, qbuf):
    q = jnp.dot(tile, wq, preferred_element_type=F32).astype(BF)
    q = q * jnp.asarray(0.125, BF)
    zero = jnp.zeros_like(q)
    for e in range(HEADS):
        qbuf[m, e * T : (e + 1) * T, :] = jnp.where(head_mask(e, q.shape), q, zero)


def geometry(mine, near, limit, i):
    mine = mine[i * ROWS : (i + 1) * ROWS, :]
    d = [mine[:, c : c + 1] - near[c : c + 1, :] for c in range(3)]
    r2 = d[0] * d[0] + d[1] * d[1] + d[2] * d[2]
    coefs = cos_half_coefs()
    poly = r2 * coefs[-1] + coefs[-2]
    for cf in coefs[-3::-1]:
        poly = poly * r2 + cf
    return r2, jnp.where(r2 < limit, poly * poly, 0.0).astype(BF)


def pair_terms(m, n, limit, decays, qbuf, kbuf, vbuf, jbuf, ibuf, macc):
    near = jbuf[n]
    mine = ibuf[m]
    k = kbuf[n]
    parts = [geometry(mine, near, limit, i) for i in range(T // ROWS)]
    cut = jnp.concatenate([part[1] for part in parts], axis=0)
    ws = []
    for e2 in range(HEADS // 2):
        half = lax.dot_general(
            qbuf[m, e2 * 2 * T : (e2 + 1) * 2 * T, :],
            k,
            (((1,), (1,)), ((), ())),
            preferred_element_type=F32,
        ).astype(BF)
        for s in range(2):
            e = e2 * 2 + s
            u = half[s * T : (s + 1) * T, :]
            power = jnp.concatenate([(part[0] * decays[e]).astype(BF) for part in parts], axis=0)
            ws.append((u + u * jnp.tanh(u)) * (jnp.exp2(power) * cut))
    macc[m] += jnp.dot(jnp.concatenate(ws, axis=1), vbuf[n], preferred_element_type=F32)


def visit(wide, slots, table, falloff, lo, hi, todo, qbuf, kbuf, vbuf, jbuf, ibuf, macc):
    count = jnp.int32(0)
    for t in range(4):
        for s in range(K):
            n = table[slots[t // 2, t % 2, s] + 1]
            todo[count] = (n - lo) * 4 + t
            count = count + jnp.where((n >= lo) & (n < hi), 1, 0)
    todo[count] = 0
    decays = [falloff[e] * (-LOG2E) for e in range(HEADS)]

    def step(i, carry):
        for s in range(wide):
            at = i * wide + s
            code = todo[jnp.minimum(at, count)]
            limit = jnp.where(at < count, 1.0, 0.0)
            n = code // 4
            pair_terms(
                code - n * 4, n, limit, decays, qbuf, kbuf, vbuf, jbuf, ibuf, macc
            )
        return carry

    lax.fori_loop(0, (count + wide - 1) // wide, step, 0)


def own_rows(p, t):
    return [p[0, c, t // 2, t % 2 : t % 2 + 1, :] for c in range(3)]


def own_columns(p, ibuf, t):
    ibuf[t] = jnp.concatenate(own_rows(p, t) + [jnp.zeros((5, T), F32)], axis=0).T


def own_body(
    slots, table, falloff, r0, r1, p, wqkv, charge, macc, qbuf, ibuf, todo, kbuf, vbuf, jbuf
):
    center = origin(p)
    for t in range(4):
        tile = (r0 if t < 2 else r1)[t % 2, 0:T, :]
        project_kv(
            tile, t, own_rows(p, t), center, wqkv[:, F:], charge_rows(charge), kbuf, vbuf, jbuf
        )
        project_q(tile, t, wqkv[:, :F], qbuf)
        own_columns(p, ibuf, t)
        macc[t] = jnp.zeros((T, 2 * F), F32)
    visit(WIDE, slots, table, falloff, 0, 4, todo, qbuf, kbuf, vbuf, jbuf, ibuf, macc)


def project_halo(halo, p, wqkv, charge, kbuf, vbuf, jbuf):
    center = origin(p)
    for i, (src, a) in enumerate(halo):
        blk = src[a, T:PR, :].astype(F32)
        rows = [
            blk[3 * c : 3 * c + 1] + blk[3 * c + 1 : 3 * c + 2] + blk[3 * c + 2 : 3 * c + 3]
            for c in range(3)
        ]
        project_kv(
            src[a, 0:T, :], i, rows, center, wqkv[:, F:], charge_rows(charge), kbuf, vbuf, jbuf
        )


def edge_body(
    slots, table, falloff, p, qbuf, ibuf, up, down, gin, macc_in, wqkv, charge,
    macc, todo, kbuf, vbuf, jbuf,
):
    halo = [(up, 0), (up, 1), (down, 0), (down, 1), (gin, 0), (gin, 1)]
    project_halo(halo, p, wqkv, charge, kbuf, vbuf, jbuf)
    for t in range(4):
        macc[t] = macc_in[t]
    visit(WIDE, slots, table, falloff, 4, 10, todo, qbuf, kbuf, vbuf, jbuf, ibuf, macc)


def charge_rows(charge):
    return jnp.broadcast_to(charge[...].astype(F32), (16, F)).astype(BF)


def rest_body(
    last,
    slots, table, falloff, headw, levels, heat, p, qbuf, ibuf, h, jit, c0, c1,
    macc_in, wqkv, wo, charge,
    *refs,
):
    if last:
        hout, pout, fout = refs[:3]
        refs = refs[3:]
    else:
        xout = refs[0]
        refs = refs[1:]
    todo, kbuf, vbuf, jbuf, macc = refs
    center = origin(p)
    project_halo([(c0, 0), (c1, 0)], p, wqkv, charge, kbuf, vbuf, jbuf)
    for t in range(4):
        macc[t] = macc_in[t]
    visit(2, slots, table, falloff, 10, 12, todo, qbuf, kbuf, vbuf, jbuf, ibuf, macc)
    scale = JITTER * jnp.sqrt(jnp.full((1, T), levels[heat[0]], F32))
    for t in range(4):
        a, b = t // 2, t % 2
        message = (macc[t, :, :F] * MESSAGE_SCALE).astype(BF)
        mixed = jnp.dot(message, wo[...], preferred_element_type=F32)
        old = h[0, a, b] if len(h.shape) == 5 else h[t]
        updated = (old.astype(F32) + mixed).astype(BF)
        if last:
            hout[0, a, b] = updated
        else:
            for q in range(4):
                xout[4 * t + q, 0:32, :] = updated[q * 32 : (q + 1) * 32, :]
        terms = macc[t, :, F:].T
        total = terms[0:HD, :] * headw[0]
        for e in range(1, HEADS):
            total = total + terms[e * HD : (e + 1) * HD, :] * headw[e]
        sums = [total[3 * c : 3 * c + 1] + total[3 * c + 1 : 3 * c + 2] + total[3 * c + 2 : 3 * c + 3] for c in range(4)]
        for c, row in enumerate(own_rows(p, t)):
            force = ((row - center[c]) * sums[0] - sums[c + 1]) * FORCE_SCALE
            moved = row + DELTA * force + scale * jit[0, c, a, b : b + 1, :]
            if last:
                pout[0, c, a, b : b + 1, :] = moved
                fout[0, c, a, b : b + 1, :] = force
            else:
                xout[4 * t + c, 32:40, :] = jnp.concatenate(
                    list(parts3(moved)) + [jnp.zeros((5, T), F32)], axis=0
                ).astype(BF)
        if not last:
            xout[4 * t + 3, 32:40, :] = jnp.zeros((8, T), BF)


def route_body(partner, x, out):
    for r in range(16):
        out[r] = x[partner[r]]


def scratch(count):
    return [
        pltpu.SMEM((4 * K + 1,), jnp.int32),
        pltpu.VMEM((count, T, F), BF),
        pltpu.VMEM((count, HEADS * T, 2 * F), BF),
        pltpu.VMEM((count, 8, T), F32),
    ]


HSHAPE = (1, 2, 2, T, F)
PSHAPE = (1, 3, 2, 2, T)


def move(last, rows, p, h, jit, slots, consts):
    r0, r1, g = rows
    table = jnp.asarray(STORED, jnp.int32)
    wqkv, wo, charge, falloff, headw, levels, heat = consts
    gx = lax.axis_size("gx")
    swap = [(0, 1), (1, 0)]
    fwd = [(i, (i + 1) % gx) for i in range(gx)]
    bwd = [((i + 1) % gx, i) for i in range(gx)]
    gin = lax.ppermute(g, "gy", swap)
    up = near(lax.ppermute(r1, "gx", fwd))
    down = near(lax.ppermute(r0, "gx", bwd))
    sums = vout((4, T, 2 * F), F32)
    macc, qbuf, ibuf = call(
        own_body,
        "own",
        (sums, vout((4, HEADS * T, F), BF), vout((4, T, 8), F32)),
        [sm()] * 3 + [vm()] * 5,
        scratch(4),
    )(slots, table, falloff, near(r0), near(r1), p, wqkv, charge)
    gin, macc = lax.optimization_barrier((gin, macc))
    c0 = lax.ppermute(gin[1:2], "gx", fwd)
    c1 = lax.ppermute(gin[0:1], "gx", bwd)
    qbuf, ibuf = near(qbuf), near(ibuf)
    macc = call(edge_body, "edge", sums, [sm()] * 3 + [vm()] * 9, scratch(6))(
        slots, table, falloff, p, qbuf, ibuf, up, down, near(gin), near(macc), wqkv, charge
    )
    c0, c1, macc = lax.optimization_barrier((c0, c1, macc))
    if last:
        outs = (sds(HSHAPE, BF), sds(PSHAPE, F32), sds(PSHAPE, F32))
    else:
        outs = vout((16, XR, F), BF)
    return call(
        lambda *refs: rest_body(last, *refs),
        "rest",
        outs,
        [sm()] * 6 + [vm()] * 11,
        scratch(2) + [pltpu.VMEM((4, T, 2 * F), F32)],
    )(
        slots, table, falloff, headw, levels, heat, p, qbuf, ibuf, h, jit, near(c0), near(c1),
        near(macc), wqkv, wo, charge,
    )


def per_device(
    descriptors, locations, jit1, jit2, slots, levels, heat, partner,
    gain, wqkv, wo, charge, falloff, headw,
):
    gain = gain.reshape(1, F)
    charge = near(charge.reshape(1, F))
    wqkv = near(wqkv)
    wo = near(wo)
    side = lax.axis_index("gy").reshape(1).astype(jnp.int32)
    consts = (wqkv, wo, charge, falloff, headw, levels, heat)
    row = vout((2, PR, F), BF)
    rows = call(
        first_body, "first", (row, row, row), [sm()] + [vm()] * 3, [pltpu.VMEM((4, 16, T), F32)]
    )(side, descriptors, locations, gain)
    x = move(False, rows, near(locations), near(descriptors), near(jit1), slots, consts)
    x = lax.all_to_all(x, "rep", split_axis=0, concat_axis=0, tiled=True)
    x = call(route_body, "route", vout((16, XR, F), BF), [sm(), vm()])(partner, near(x))
    x = lax.all_to_all(x, "rep", split_axis=0, concat_axis=0, tiled=True)
    r0, r1, g, h1, p1 = call(
        second_body,
        "second",
        (row, row, row, vout((4, T, F), BF), vout(PSHAPE, F32)),
        [sm()] + [vm()] * 2,
        [pltpu.VMEM((4, 16, T), F32)],
    )(side, near(x), near(gain))
    return move(True, (r0, r1, g), near(p1), near(h1), near(jit2), slots, consts)


def solution(mesh):
    in_specs = (
        P("rep", "gx", "gy", None, None),
        P("rep", None, "gx", "gy", None),
        P("rep", None, "gx", "gy", None),
        P("rep", None, "gx", "gy", None),
        P("gx", "gy", None),
        P(),
        P("rep"),
        P(),
        P(),
        P(),
        P(),
        P(),
        P(),
        P(),
    )
    out_specs = (
        P("rep", "gx", "gy", None, None),
        P("rep", None, "gx", "gy", None),
        P("rep", None, "gx", "gy", None),
    )
    return jax.shard_map(
        per_device, mesh=mesh, in_specs=in_specs, out_specs=out_specs, check_vma=False
    )
```

```python
import math

import jax
import jax.numpy as jnp
from jax import lax
from jax.experimental import pallas as pl
from jax.experimental.pallas import tpu as pltpu
from jax.sharding import PartitionSpec as P

F = 128
HEADS = 8
HD = 16
T = 128
K = 6
PR = T + 16
XR = 40
NORM_EPS = 1e-05
DELTA = 0.1
JITTER = 0.05
MESSAGE_SCALE = 1.0 / 32.0
FORCE_SCALE = 1.0 / 16.0
LOG2E = 1.4426950408889634
ROWS = T
WIDE = 3
STORED = (-1, 10, 4, 5, 10, 8, 0, 1, 8, 9, 2, 3, 9, 11, 6, 7, 11)
INTERPRET = False

BF = jnp.bfloat16
F32 = jnp.float32


def cos_half_coefs():
    return (
        0.9999999997799036,
        -1.2337005342697012,
        0.2536693224722507,
        -0.020862687547626383,
        0.000917723882055615,
        -2.3824535481836604e-05,
    )


def call(body, name, out_shape, in_specs, scratch=()):
    many = isinstance(out_shape, tuple)
    out_specs = (vm(),) * len(out_shape) if many else vm()
    return pl.pallas_call(
        body,
        name=name,
        out_shape=out_shape,
        in_specs=in_specs,
        out_specs=out_specs,
        scratch_shapes=scratch,
        compiler_params=pltpu.CompilerParams(vmem_limit_bytes=20 * 1024 * 1024),
        interpret=INTERPRET,
    )


def near(x):
    return x if INTERPRET else pltpu.with_memory_space_constraint(x, pltpu.VMEM)


def far(x):
    return x if INTERPRET else pltpu.with_memory_space_constraint(x, pltpu.HBM)


def sds(shape, dtype):
    return jax.ShapeDtypeStruct(shape, dtype)


def vout(shape, dtype):
    return sds(shape, dtype) if INTERPRET else pltpu.VMEM(shape, dtype)


def vm():
    return pl.BlockSpec(memory_space=pltpu.VMEM)


def sm():
    return pl.BlockSpec(memory_space=pltpu.SMEM)


def parts3(x):
    hi = x.astype(BF).astype(F32)
    rest = x - hi
    mid = rest.astype(BF).astype(F32)
    lo = rest - mid
    return hi, mid, lo


def norm_rows(h, gain):
    x = h.astype(F32)
    mean = jnp.mean(x, axis=-1, keepdims=True)
    xc = x - mean
    var = jnp.mean(xc * xc, axis=-1, keepdims=True)
    return (xc * lax.rsqrt(var + NORM_EPS) * gain).astype(BF)


def emit_rows(side, tiles, coords, r0, r1, g, cbuf):
    blocks = []
    for t in range(4):
        cbuf[t] = jnp.zeros((16, T), F32)
        for c in range(3):
            for k, part in enumerate(parts3(coords(c, t))):
                cbuf[t, c * 3 + k : c * 3 + k + 1, :] = part
        blocks.append(cbuf[t].astype(BF))
    for t in range(4):
        dst = r0 if t < 2 else r1
        dst[t % 2, 0:T, :] = tiles[t]
        dst[t % 2, T:PR, :] = blocks[t]
    for la in range(2):
        pick = side == 0
        g[la, 0:T, :] = jnp.where(pick, tiles[2 * la + 1], tiles[2 * la])
        g[la, T:PR, :] = jnp.where(pick, blocks[2 * la + 1], blocks[2 * la])


def first_body(side, h, p, gain, r0, r1, g, cbuf):
    tiles = [norm_rows(h[0, t // 2, t % 2], gain[...]) for t in range(4)]
    emit_rows(side[0], tiles, lambda c, t: own_rows(p, t)[c], r0, r1, g, cbuf)


def second_body(side, x, gain, r0, r1, g, h, p, cbuf):
    for t in range(4):
        for c in range(3):
            blk = x[4 * t + c, 32:40, :].astype(F32)
            p[0, c, t // 2, t % 2 : t % 2 + 1, :] = blk[0:1] + blk[1:2] + blk[2:3]
        for q in range(4):
            h[t, q * 32 : (q + 1) * 32, :] = x[4 * t + q, 0:32, :]
    tiles = [norm_rows(h[t], gain[...]) for t in range(4)]
    emit_rows(side[0], tiles, lambda c, t: own_rows(p, t)[c], r0, r1, g, cbuf)


def head_mask(e, shape):
    lane = lax.broadcasted_iota(jnp.int32, shape, 1)
    return (lane & (F - 1)) // HD == e


def origin(p):
    return [p[0, c, 0, 0:1, 0:1] for c in range(3)]


def project_kv(tile, n, rows, center, wkv, charge, kbuf, vbuf, jbuf):
    kv = jnp.dot(tile, wkv, preferred_element_type=F32)
    k = kv[:, :F].astype(BF)
    kbuf[n] = k
    probe = lax.dot_general(charge, k, (((1,), (1,)), ((), ())), preferred_element_type=F32)[0:1]
    terms = [probe] + [probe * (rows[c] - center[c]) for c in range(3)]
    stack = [part for term in terms for part in parts3(term)] + [jnp.zeros((4, T), F32)]
    force = jnp.concatenate(stack, axis=0)
    force = jnp.concatenate([force] * HEADS, axis=0).T
    both = jnp.concatenate([kv[:, F:], force], axis=1).astype(BF)
    zero = jnp.zeros_like(both)
    for e in range(HEADS):
        vbuf[n, e * T : (e + 1) * T, :] = jnp.where(head_mask(e, both.shape), both, zero)
    jbuf[n] = jnp.concatenate(list(rows) + [jnp.zeros((5, T), F32)], axis=0)


def project_q(tile, m, wq, qbuf):
    q = jnp.dot(tile, wq, preferred_element_type=F32).astype(BF)
    q = q * jnp.asarray(0.125, BF)
    zero = jnp.zeros_like(q)
    for e in range(HEADS):
        qbuf[m, e * T : (e + 1) * T, :] = jnp.where(head_mask(e, q.shape), q, zero)


def geometry(mine, near, limit, i):
    mine = mine[i * ROWS : (i + 1) * ROWS, :]
    d = [mine[:, c : c + 1] - near[c : c + 1, :] for c in range(3)]
    r2 = d[0] * d[0] + d[1] * d[1] + d[2] * d[2]
    coefs = cos_half_coefs()
    poly = r2 * coefs[-1] + coefs[-2]
    for cf in coefs[-3::-1]:
        poly = poly * r2 + cf
    return r2, jnp.where(r2 < limit, poly * poly, 0.0).astype(BF)


def pair_terms(m, n, limit, decays, qbuf, kbuf, vbuf, jbuf, ibuf, macc):
    near = jbuf[n]
    mine = ibuf[m]
    k = kbuf[n]
    parts = [geometry(mine, near, limit, i) for i in range(T // ROWS)]
    cut = jnp.concatenate([part[1] for part in parts], axis=0)
    ws = []
    for e2 in range(HEADS // 2):
        half = lax.dot_general(
            qbuf[m, e2 * 2 * T : (e2 + 1) * 2 * T, :],
            k,
            (((1,), (1,)), ((), ())),
            preferred_element_type=F32,
        ).astype(BF)
        for s in range(2):
            e = e2 * 2 + s
            u = half[s * T : (s + 1) * T, :]
            power = jnp.concatenate([(part[0] * decays[e]).astype(BF) for part in parts], axis=0)
            ws.append((u + u * jnp.tanh(u)) * (jnp.exp2(power) * cut))
    macc[m] += jnp.dot(jnp.concatenate(ws, axis=1), vbuf[n], preferred_element_type=F32)


def visit(wide, slots, table, falloff, lo, hi, todo, qbuf, kbuf, vbuf, jbuf, ibuf, macc):
    count = jnp.int32(0)
    for t in range(4):
        for s in range(K):
            n = table[slots[t // 2, t % 2, s] + 1]
            todo[count] = (n - lo) * 4 + t
            count = count + jnp.where((n >= lo) & (n < hi), 1, 0)
    todo[count] = 0
    decays = [falloff[e] * (-LOG2E) for e in range(HEADS)]

    def step(i, carry):
        for s in range(wide):
            at = i * wide + s
            code = todo[jnp.minimum(at, count)]
            limit = jnp.where(at < count, 1.0, 0.0)
            n = code // 4
            pair_terms(
                code - n * 4, n, limit, decays, qbuf, kbuf, vbuf, jbuf, ibuf, macc
            )
        return carry

    lax.fori_loop(0, (count + wide - 1) // wide, step, 0)


def own_rows(p, t):
    return [p[0, c, t // 2, t % 2 : t % 2 + 1, :] for c in range(3)]


def own_columns(p, ibuf, t):
    ibuf[t] = jnp.concatenate(own_rows(p, t) + [jnp.zeros((5, T), F32)], axis=0).T


def own_body(
    slots, table, falloff, r0, r1, p, wqkv, charge, macc, qbuf, ibuf, todo, kbuf, vbuf, jbuf
):
    center = origin(p)
    for t in range(4):
        tile = (r0 if t < 2 else r1)[t % 2, 0:T, :]
        project_kv(
            tile, t, own_rows(p, t), center, wqkv[:, F:], charge_rows(charge), kbuf, vbuf, jbuf
        )
        project_q(tile, t, wqkv[:, :F], qbuf)
        own_columns(p, ibuf, t)
        macc[t] = jnp.zeros((T, 2 * F), F32)
    visit(WIDE, slots, table, falloff, 0, 4, todo, qbuf, kbuf, vbuf, jbuf, ibuf, macc)


def project_halo(halo, p, wqkv, charge, kbuf, vbuf, jbuf):
    center = origin(p)
    for i, (src, a) in enumerate(halo):
        blk = src[a, T:PR, :].astype(F32)
        rows = [
            blk[3 * c : 3 * c + 1] + blk[3 * c + 1 : 3 * c + 2] + blk[3 * c + 2 : 3 * c + 3]
            for c in range(3)
        ]
        project_kv(
            src[a, 0:T, :], i, rows, center, wqkv[:, F:], charge_rows(charge), kbuf, vbuf, jbuf
        )


def edge_body(
    slots, table, falloff, p, qbuf, ibuf, up, down, gin, macc_in, wqkv, charge,
    macc, todo, kbuf, vbuf, jbuf,
):
    halo = [(up, 0), (up, 1), (down, 0), (down, 1), (gin, 0), (gin, 1)]
    project_halo(halo, p, wqkv, charge, kbuf, vbuf, jbuf)
    for t in range(4):
        macc[t] = macc_in[t]
    visit(WIDE, slots, table, falloff, 4, 10, todo, qbuf, kbuf, vbuf, jbuf, ibuf, macc)


def charge_rows(charge):
    return jnp.broadcast_to(charge[...].astype(F32), (16, F)).astype(BF)


def rest_body(
    last,
    slots, table, falloff, headw, levels, heat, p, qbuf, ibuf, h, jit, c0, c1,
    macc_in, wqkv, wo, charge,
    *refs,
):
    if last:
        hout, pout, fout = refs[:3]
        refs = refs[3:]
    else:
        xout = refs[0]
        refs = refs[1:]
    todo, kbuf, vbuf, jbuf, macc = refs
    center = origin(p)
    project_halo([(c0, 1), (c1, 0)], p, wqkv, charge, kbuf, vbuf, jbuf)
    for t in range(4):
        macc[t] = macc_in[t]
    visit(2, slots, table, falloff, 10, 12, todo, qbuf, kbuf, vbuf, jbuf, ibuf, macc)
    scale = JITTER * jnp.sqrt(jnp.full((1, T), levels[heat[0]], F32))
    for t in range(4):
        a, b = t // 2, t % 2
        message = (macc[t, :, :F] * MESSAGE_SCALE).astype(BF)
        mixed = jnp.dot(message, wo[...], preferred_element_type=F32)
        old = h[0, a, b] if len(h.shape) == 5 else h[t]
        updated = (old.astype(F32) + mixed).astype(BF)
        if last:
            hout[0, a, b] = updated
        else:
            for q in range(4):
                xout[4 * t + q, 0:32, :] = updated[q * 32 : (q + 1) * 32, :]
        terms = macc[t, :, F:].T
        total = terms[0:HD, :] * headw[0]
        for e in range(1, HEADS):
            total = total + terms[e * HD : (e + 1) * HD, :] * headw[e]
        sums = [total[3 * c : 3 * c + 1] + total[3 * c + 1 : 3 * c + 2] + total[3 * c + 2 : 3 * c + 3] for c in range(4)]
        for c, row in enumerate(own_rows(p, t)):
            force = ((row - center[c]) * sums[0] - sums[c + 1]) * FORCE_SCALE
            moved = row + DELTA * force + scale * jit[0, c, a, b : b + 1, :]
            if last:
                pout[0, c, a, b : b + 1, :] = moved
                fout[0, c, a, b : b + 1, :] = force
            else:
                xout[4 * t + c, 32:40, :] = jnp.concatenate(
                    list(parts3(moved)) + [jnp.zeros((5, T), F32)], axis=0
                ).astype(BF)
        if not last:
            xout[4 * t + 3, 32:40, :] = jnp.zeros((8, T), BF)


def route_body(partner, x, out):
    for r in range(16):
        out[r] = x[partner[r]]


def scratch(count):
    return [
        pltpu.SMEM((4 * K + 1,), jnp.int32),
        pltpu.VMEM((count, T, F), BF),
        pltpu.VMEM((count, HEADS * T, 2 * F), BF),
        pltpu.VMEM((count, 8, T), F32),
    ]


HSHAPE = (1, 2, 2, T, F)
PSHAPE = (1, 3, 2, 2, T)


def move(last, rows, p, h, jit, slots, consts):
    r0, r1, g = rows
    table = jnp.asarray(STORED, jnp.int32)
    wqkv, wo, charge, falloff, headw, levels, heat = consts
    gx = lax.axis_size("gx")
    swap = [(0, 1), (1, 0)]
    fwd = [(i, (i + 1) % gx) for i in range(gx)]
    bwd = [((i + 1) % gx, i) for i in range(gx)]
    gin = lax.ppermute(g, "gy", swap)
    up = near(lax.ppermute(r1, "gx", fwd))
    down = near(lax.ppermute(r0, "gx", bwd))
    sums = vout((4, T, 2 * F), F32)
    macc, qbuf, ibuf = call(
        own_body,
        "own",
        (sums, vout((4, HEADS * T, F), BF), vout((4, T, 8), F32)),
        [sm()] * 3 + [vm()] * 5,
        scratch(4),
    )(slots, table, falloff, near(r0), near(r1), p, wqkv, charge)
    gin, macc = lax.optimization_barrier((gin, macc))
    c0 = lax.ppermute(gin, "gx", fwd)
    c1 = lax.ppermute(gin, "gx", bwd)
    qbuf, ibuf = near(qbuf), near(ibuf)
    macc = call(edge_body, "edge", sums, [sm()] * 3 + [vm()] * 9, scratch(6))(
        slots, table, falloff, p, qbuf, ibuf, up, down, near(gin), near(macc), wqkv, charge
    )
    c0, c1, macc = lax.optimization_barrier((c0, c1, macc))
    if last:
        outs = (sds(HSHAPE, BF), sds(PSHAPE, F32), sds(PSHAPE, F32))
    else:
        outs = vout((16, XR, F), BF)
    return call(
        lambda *refs: rest_body(last, *refs),
        "rest",
        outs,
        [sm()] * 6 + [vm()] * 11,
        scratch(2) + [pltpu.VMEM((4, T, 2 * F), F32)],
    )(
        slots, table, falloff, headw, levels, heat, p, qbuf, ibuf, h, jit, near(c0), near(c1),
        near(macc), wqkv, wo, charge,
    )


def per_device(
    descriptors, locations, jit1, jit2, slots, levels, heat, partner,
    gain, wqkv, wo, charge, falloff, headw,
):
    gain = gain.reshape(1, F)
    charge = near(charge.reshape(1, F))
    wqkv = near(wqkv)
    wo = near(wo)
    side = lax.axis_index("gy").reshape(1).astype(jnp.int32)
    consts = (wqkv, wo, charge, falloff, headw, levels, heat)
    row = vout((2, PR, F), BF)
    rows = call(
        first_body, "first", (row, row, row), [sm()] + [vm()] * 3, [pltpu.VMEM((4, 16, T), F32)]
    )(side, far(descriptors), far(locations), far(gain))
    x = move(False, rows, near(locations), near(descriptors), near(jit1), slots, consts)
    x = lax.all_to_all(x, "rep", split_axis=0, concat_axis=0, tiled=True)
    x = call(route_body, "route", vout((16, XR, F), BF), [sm(), vm()])(partner, near(x))
    x = lax.all_to_all(x, "rep", split_axis=0, concat_axis=0, tiled=True)
    r0, r1, g, h1, p1 = call(
        second_body,
        "second",
        (row, row, row, vout((4, T, F), BF), vout(PSHAPE, F32)),
        [sm()] + [vm()] * 2,
        [pltpu.VMEM((4, 16, T), F32)],
    )(side, near(x), near(gain))
    return move(True, (r0, r1, g), near(p1), near(h1), near(jit2), slots, consts)


def solution(mesh):
    in_specs = (
        P("rep", "gx", "gy", None, None),
        P("rep", None, "gx", "gy", None),
        P("rep", None, "gx", "gy", None),
        P("rep", None, "gx", "gy", None),
        P("gx", "gy", None),
        P(),
        P("rep"),
        P(),
        P(),
        P(),
        P(),
        P(),
        P(),
        P(),
    )
    out_specs = (
        P("rep", "gx", "gy", None, None),
        P("rep", None, "gx", "gy", None),
        P("rep", None, "gx", "gy", None),
    )
    return jax.shard_map(
        per_device, mesh=mesh, in_specs=in_specs, out_specs=out_specs, check_vma=False
    )
```

```python
import math

import jax
import jax.numpy as jnp
from jax import lax
from jax.experimental import pallas as pl
from jax.experimental.pallas import tpu as pltpu
from jax.sharding import PartitionSpec as P

F = 128
HEADS = 8
HD = 16
T = 128
K = 6
PR = T + 16
XR = 40
NORM_EPS = 1e-05
DELTA = 0.1
JITTER = 0.05
MESSAGE_SCALE = 1.0 / 32.0
FORCE_SCALE = 1.0 / 16.0
LOG2E = 1.4426950408889634
ROWS = T
WIDE = 4
GROUP = 4
STORED = (-1, 10, 4, 5, 10, 8, 0, 1, 8, 9, 2, 3, 9, 11, 6, 7, 11)
INTERPRET = False

BF = jnp.bfloat16
F32 = jnp.float32


def cos_half_coefs():
    return (
        0.9999999997799036,
        -1.2337005342697012,
        0.2536693224722507,
        -0.020862687547626383,
        0.000917723882055615,
        -2.3824535481836604e-05,
    )


def call(body, name, out_shape, in_specs, scratch=()):
    many = isinstance(out_shape, tuple)
    out_specs = (vm(),) * len(out_shape) if many else vm()
    return pl.pallas_call(
        body,
        name=name,
        out_shape=out_shape,
        in_specs=in_specs,
        out_specs=out_specs,
        scratch_shapes=scratch,
        compiler_params=pltpu.CompilerParams(vmem_limit_bytes=20 * 1024 * 1024),
        interpret=INTERPRET,
    )


def near(x):
    return x if INTERPRET else pltpu.with_memory_space_constraint(x, pltpu.VMEM)


def far(x):
    return x if INTERPRET else pltpu.with_memory_space_constraint(x, pltpu.HBM)


def sds(shape, dtype):
    return jax.ShapeDtypeStruct(shape, dtype)


def vout(shape, dtype):
    return sds(shape, dtype) if INTERPRET else pltpu.VMEM(shape, dtype)


def vm():
    return pl.BlockSpec(memory_space=pltpu.VMEM)


def sm():
    return pl.BlockSpec(memory_space=pltpu.SMEM)


def parts3(x):
    hi = x.astype(BF).astype(F32)
    rest = x - hi
    mid = rest.astype(BF).astype(F32)
    lo = rest - mid
    return hi, mid, lo


def norm_rows(h, gain):
    x = h.astype(F32)
    mean = jnp.mean(x, axis=-1, keepdims=True)
    xc = x - mean
    var = jnp.mean(xc * xc, axis=-1, keepdims=True)
    return (xc * lax.rsqrt(var + NORM_EPS) * gain).astype(BF)


def emit_rows(side, tiles, coords, r0, r1, g, cbuf):
    blocks = []
    for t in range(4):
        cbuf[t] = jnp.zeros((16, T), F32)
        for c in range(3):
            for k, part in enumerate(parts3(coords(c, t))):
                cbuf[t, c * 3 + k : c * 3 + k + 1, :] = part
        blocks.append(cbuf[t].astype(BF))
    for t in range(4):
        dst = r0 if t < 2 else r1
        dst[t % 2, 0:T, :] = tiles[t]
        dst[t % 2, T:PR, :] = blocks[t]
    for la in range(2):
        pick = side == 0
        g[la, 0:T, :] = jnp.where(pick, tiles[2 * la + 1], tiles[2 * la])
        g[la, T:PR, :] = jnp.where(pick, blocks[2 * la + 1], blocks[2 * la])


def first_body(side, h, p, gain, r0, r1, g, cbuf):
    tiles = [norm_rows(h[0, t // 2, t % 2], gain[...]) for t in range(4)]
    emit_rows(side[0], tiles, lambda c, t: own_rows(p, t)[c], r0, r1, g, cbuf)


def second_body(side, x, gain, r0, r1, g, h, p, cbuf):
    for t in range(4):
        for c in range(3):
            blk = x[4 * t + c, 32:40, :].astype(F32)
            p[0, c, t // 2, t % 2 : t % 2 + 1, :] = blk[0:1] + blk[1:2] + blk[2:3]
        for q in range(4):
            h[t, q * 32 : (q + 1) * 32, :] = x[4 * t + q, 0:32, :]
    tiles = [norm_rows(h[t], gain[...]) for t in range(4)]
    emit_rows(side[0], tiles, lambda c, t: own_rows(p, t)[c], r0, r1, g, cbuf)


def head_mask(e, shape):
    lane = lax.broadcasted_iota(jnp.int32, shape, 1)
    return (lane & (F - 1)) // HD == e


def origin(p):
    return [p[0, c, 0, 0:1, 0:1] for c in range(3)]


def project_kv(tile, n, rows, center, wkv, charge, kbuf, vbuf, jbuf):
    kv = jnp.dot(tile, wkv, preferred_element_type=F32)
    columns = kv[:, :F].T.astype(BF)
    kbuf[n] = columns
    probe = jnp.dot(charge, columns, preferred_element_type=F32)[0:1]
    terms = [probe] + [probe * (rows[c] - center[c]) for c in range(3)]
    stack = [part for term in terms for part in parts3(term)] + [jnp.zeros((4, T), F32)]
    force = jnp.concatenate(stack, axis=0)
    force = jnp.concatenate([force] * HEADS, axis=0).T
    both = jnp.concatenate([kv[:, F:], force], axis=1).astype(BF)
    zero = jnp.zeros_like(both)
    for e in range(HEADS):
        vbuf[n, e * T : (e + 1) * T, :] = jnp.where(head_mask(e, both.shape), both, zero)
    jbuf[n] = jnp.concatenate(list(rows) + [jnp.zeros((5, T), F32)], axis=0)


def project_q(tile, m, wq, qbuf):
    q = jnp.dot(tile, wq, preferred_element_type=F32).astype(BF)
    q = q * jnp.asarray(0.125, BF)
    zero = jnp.zeros_like(q)
    for e in range(HEADS):
        qbuf[m, e * T : (e + 1) * T, :] = jnp.where(head_mask(e, q.shape), q, zero)


def geometry(mine, near, limit, i):
    mine = mine[i * ROWS : (i + 1) * ROWS, :]
    d = [mine[:, c : c + 1] - near[c : c + 1, :] for c in range(3)]
    r2 = d[0] * d[0] + d[1] * d[1] + d[2] * d[2]
    coefs = cos_half_coefs()
    poly = r2 * coefs[-1] + coefs[-2]
    for cf in coefs[-3::-1]:
        poly = poly * r2 + cf
    return r2, jnp.where(r2 < limit, poly * poly, 0.0).astype(BF)


def pair_terms(m, n, limit, decays, qbuf, kbuf, vbuf, jbuf, ibuf, macc):
    near = jbuf[n]
    mine = ibuf[m]
    k = kbuf[n]
    parts = [geometry(mine, near, limit, i) for i in range(T // ROWS)]
    cut = jnp.concatenate([part[1] for part in parts], axis=0)
    ws = []
    for group in range(HEADS // GROUP):
        half = jnp.dot(
            qbuf[m, group * GROUP * T : (group + 1) * GROUP * T, :],
            k,
            preferred_element_type=F32,
        ).astype(BF)
        for s in range(GROUP):
            e = group * GROUP + s
            u = half[s * T : (s + 1) * T, :]
            power = jnp.concatenate([(part[0] * decays[e]).astype(BF) for part in parts], axis=0)
            ws.append((u + u * jnp.tanh(u)) * (jnp.exp2(power) * cut))
    macc[m] += jnp.dot(jnp.concatenate(ws, axis=1), vbuf[n], preferred_element_type=F32)


def visit(wide, slots, table, falloff, todo, qbuf, kbuf, vbuf, jbuf, ibuf, macc):
    count = jnp.int32(0)
    for t in range(4):
        for s in range(K):
            code = table[slots[t // 2, t % 2, s] + 1]
            todo[count] = code + t
            count = count + jnp.where(code >= 0, 1, 0)
    todo[count] = 0
    decays = [falloff[e] * (-LOG2E) for e in range(HEADS)]

    def step(i, carry):
        for s in range(wide):
            at = i * wide + s
            code = todo[jnp.minimum(at, count)]
            limit = jnp.where(at < count, 1.0, 0.0)
            n = code // 4
            pair_terms(
                code - n * 4, n, limit, decays, qbuf, kbuf, vbuf, jbuf, ibuf, macc
            )
        return carry

    lax.fori_loop(0, (count + wide - 1) // wide, step, 0)


def own_rows(p, t):
    return [p[0, c, t // 2, t % 2 : t % 2 + 1, :] for c in range(3)]


def own_columns(p, ibuf, t):
    ibuf[t] = jnp.concatenate(own_rows(p, t) + [jnp.zeros((5, T), F32)], axis=0).T


def own_body(
    slots, table, falloff, r0, r1, p, wqkv, charge, macc, qbuf, ibuf, todo, kbuf, vbuf, jbuf
):
    center = origin(p)
    for t in range(4):
        tile = (r0 if t < 2 else r1)[t % 2, 0:T, :]
        project_kv(
            tile, t, own_rows(p, t), center, wqkv[:, F:], charge_rows(charge), kbuf, vbuf, jbuf
        )
        project_q(tile, t, wqkv[:, :F], qbuf)
        own_columns(p, ibuf, t)
        macc[t] = jnp.zeros((T, 2 * F), F32)
    visit(WIDE, slots, table, falloff, todo, qbuf, kbuf, vbuf, jbuf, ibuf, macc)


def project_halo(halo, p, wqkv, charge, kbuf, vbuf, jbuf):
    center = origin(p)
    for i, (src, a) in enumerate(halo):
        blk = src[a, T:PR, :].astype(F32)
        rows = [
            blk[3 * c : 3 * c + 1] + blk[3 * c + 1 : 3 * c + 2] + blk[3 * c + 2 : 3 * c + 3]
            for c in range(3)
        ]
        project_kv(
            src[a, 0:T, :], i, rows, center, wqkv[:, F:], charge_rows(charge), kbuf, vbuf, jbuf
        )


def edge_body(
    slots, table, falloff, p, qbuf, ibuf, up, down, gin, macc_in, wqkv, charge,
    macc, todo, kbuf, vbuf, jbuf,
):
    halo = [(up, 0), (up, 1), (down, 0), (down, 1), (gin, 0), (gin, 1)]
    project_halo(halo, p, wqkv, charge, kbuf, vbuf, jbuf)
    for t in range(4):
        macc[t] = macc_in[t]
    visit(WIDE, slots, table, falloff, todo, qbuf, kbuf, vbuf, jbuf, ibuf, macc)


def charge_rows(charge):
    return jnp.broadcast_to(charge[...].astype(F32), (16, F)).astype(BF)


def rest_body(
    last,
    slots, table, falloff, headw, levels, heat, p, qbuf, ibuf, h, jit, c0, c1,
    macc_in, wqkv, wo, charge,
    *refs,
):
    if last:
        hout, pout, fout = refs[:3]
        refs = refs[3:]
    else:
        xout = refs[0]
        refs = refs[1:]
    todo, kbuf, vbuf, jbuf, macc = refs
    center = origin(p)
    project_halo([(c0, 1), (c1, 0)], p, wqkv, charge, kbuf, vbuf, jbuf)
    for t in range(4):
        macc[t] = macc_in[t]
    visit(2, slots, table, falloff, todo, qbuf, kbuf, vbuf, jbuf, ibuf, macc)
    scale = JITTER * jnp.sqrt(jnp.full((1, T), levels[heat[0]], F32))
    for t in range(4):
        a, b = t // 2, t % 2
        message = (macc[t, :, :F] * MESSAGE_SCALE).astype(BF)
        mixed = jnp.dot(message, wo[...], preferred_element_type=F32)
        old = h[0, a, b] if len(h.shape) == 5 else h[t]
        updated = (old.astype(F32) + mixed).astype(BF)
        if last:
            hout[0, a, b] = updated
        else:
            for q in range(4):
                xout[4 * t + q, 0:32, :] = updated[q * 32 : (q + 1) * 32, :]
        terms = macc[t, :, F:].T
        total = terms[0:HD, :] * headw[0]
        for e in range(1, HEADS):
            total = total + terms[e * HD : (e + 1) * HD, :] * headw[e]
        sums = [total[3 * c : 3 * c + 1] + total[3 * c + 1 : 3 * c + 2] + total[3 * c + 2 : 3 * c + 3] for c in range(4)]
        for c, row in enumerate(own_rows(p, t)):
            force = ((row - center[c]) * sums[0] - sums[c + 1]) * FORCE_SCALE
            moved = row + DELTA * force + scale * jit[0, c, a, b : b + 1, :]
            if last:
                pout[0, c, a, b : b + 1, :] = moved
                fout[0, c, a, b : b + 1, :] = force
            else:
                xout[4 * t + c, 32:40, :] = jnp.concatenate(
                    list(parts3(moved)) + [jnp.zeros((5, T), F32)], axis=0
                ).astype(BF)
        if not last:
            xout[4 * t + 3, 32:40, :] = jnp.zeros((8, T), BF)


def route_body(partner, x, out):
    for r in range(16):
        out[r] = x[partner[r]]


def scratch(count):
    return [
        pltpu.SMEM((4 * K + 1,), jnp.int32),
        pltpu.VMEM((count, T, F), BF),
        pltpu.VMEM((count, HEADS * T, 2 * F), BF),
        pltpu.VMEM((count, 8, T), F32),
    ]


HSHAPE = (1, 2, 2, T, F)
PSHAPE = (1, 3, 2, 2, T)


def move(last, rows, p, h, jit, slots, consts):
    r0, r1, g = rows
    inside, edges, corners = (
        jnp.asarray([(n - lo) * 4 if lo <= n < hi else -4 for n in STORED], jnp.int32)
        for lo, hi in ((0, 4), (4, 10), (10, 12))
    )
    wqkv, wo, charge, falloff, headw, levels, heat = consts
    gx = lax.axis_size("gx")
    swap = [(0, 1), (1, 0)]
    fwd = [(i, (i + 1) % gx) for i in range(gx)]
    bwd = [((i + 1) % gx, i) for i in range(gx)]
    gin = lax.ppermute(g, "gy", swap)
    up = near(lax.ppermute(r1, "gx", fwd))
    down = near(lax.ppermute(r0, "gx", bwd))
    sums = vout((4, T, 2 * F), F32)
    macc, qbuf, ibuf = call(
        own_body,
        "own",
        (sums, vout((4, HEADS * T, F), BF), vout((4, T, 8), F32)),
        [sm()] * 3 + [vm()] * 5,
        scratch(4),
    )(slots, inside, falloff, near(r0), near(r1), p, wqkv, charge)
    gin, macc = lax.optimization_barrier((gin, macc))
    c0 = lax.ppermute(gin, "gx", fwd)
    c1 = lax.ppermute(gin, "gx", bwd)
    qbuf, ibuf = near(qbuf), near(ibuf)
    macc = call(edge_body, "edge", sums, [sm()] * 3 + [vm()] * 9, scratch(6))(
        slots, edges, falloff, p, qbuf, ibuf, up, down, near(gin), near(macc), wqkv, charge
    )
    c0, c1, macc = lax.optimization_barrier((c0, c1, macc))
    if last:
        outs = (sds(HSHAPE, BF), sds(PSHAPE, F32), sds(PSHAPE, F32))
    else:
        outs = vout((16, XR, F), BF)
    return call(
        lambda *refs: rest_body(last, *refs),
        "rest",
        outs,
        [sm()] * 6 + [vm()] * 11,
        scratch(2) + [pltpu.VMEM((4, T, 2 * F), F32)],
    )(
        slots, corners, falloff, headw, levels, heat, p, qbuf, ibuf, h, jit, near(c0), near(c1),
        near(macc), wqkv, wo, charge,
    )


def per_device(
    descriptors, locations, jit1, jit2, slots, levels, heat, partner,
    gain, wqkv, wo, charge, falloff, headw,
):
    gain = gain.reshape(1, F)
    charge = near(charge.reshape(1, F))
    wqkv = near(wqkv)
    wo = near(wo)
    side = lax.axis_index("gy").reshape(1).astype(jnp.int32)
    consts = (wqkv, wo, charge, falloff, headw, levels, heat)
    row = vout((2, PR, F), BF)
    rows = call(
        first_body, "first", (row, row, row), [sm()] + [vm()] * 3, [pltpu.VMEM((4, 16, T), F32)]
    )(side, far(descriptors), far(locations), far(gain))
    x = move(False, rows, near(locations), near(descriptors), near(jit1), slots, consts)
    x = lax.all_to_all(x, "rep", split_axis=0, concat_axis=0, tiled=True)
    x = call(route_body, "route", vout((16, XR, F), BF), [sm(), vm()])(partner, near(x))
    x = lax.all_to_all(x, "rep", split_axis=0, concat_axis=0, tiled=True)
    r0, r1, g, h1, p1 = call(
        second_body,
        "second",
        (row, row, row, vout((4, T, F), BF), vout(PSHAPE, F32)),
        [sm()] + [vm()] * 2,
        [pltpu.VMEM((4, 16, T), F32)],
    )(side, near(x), near(gain))
    return move(True, (r0, r1, g), near(p1), near(h1), near(jit2), slots, consts)


def solution(mesh):
    in_specs = (
        P("rep", "gx", "gy", None, None),
        P("rep", None, "gx", "gy", None),
        P("rep", None, "gx", "gy", None),
        P("rep", None, "gx", "gy", None),
        P("gx", "gy", None),
        P(),
        P("rep"),
        P(),
        P(),
        P(),
        P(),
        P(),
        P(),
        P(),
    )
    out_specs = (
        P("rep", "gx", "gy", None, None),
        P("rep", None, "gx", "gy", None),
        P("rep", None, "gx", "gy", None),
    )
    return jax.shard_map(
        per_device, mesh=mesh, in_specs=in_specs, out_specs=out_specs, check_vma=False
    )
```

```python
import math

import jax
import jax.numpy as jnp
from jax import lax
from jax.experimental import pallas as pl
from jax.experimental.pallas import tpu as pltpu
from jax.sharding import PartitionSpec as P

F = 128
HEADS = 8
HD = 16
T = 128
K = 6
PR = T + 16
XR = 40
NORM_EPS = 1e-05
DELTA = 0.1
JITTER = 0.05
MESSAGE_SCALE = 1.0 / 32.0
FORCE_SCALE = 1.0 / 16.0
LOG2E = 1.4426950408889634
ROWS = T
WIDE = 3
OWN_WIDE = 4
STORED = (-1, 10, 4, 5, 10, 8, 0, 1, 8, 9, 2, 3, 9, 11, 6, 7, 11)
INTERPRET = False

BF = jnp.bfloat16
F32 = jnp.float32


def cos_half_coefs():
    return (
        0.9999999997799036,
        -1.2337005342697012,
        0.2536693224722507,
        -0.020862687547626383,
        0.000917723882055615,
        -2.3824535481836604e-05,
    )


def call(body, name, out_shape, in_specs, scratch=()):
    many = isinstance(out_shape, tuple)
    out_specs = (vm(),) * len(out_shape) if many else vm()
    return pl.pallas_call(
        body,
        name=name,
        out_shape=out_shape,
        in_specs=in_specs,
        out_specs=out_specs,
        scratch_shapes=scratch,
        compiler_params=pltpu.CompilerParams(vmem_limit_bytes=20 * 1024 * 1024),
        interpret=INTERPRET,
    )


def near(x):
    return x if INTERPRET else pltpu.with_memory_space_constraint(x, pltpu.VMEM)


def far(x):
    return x if INTERPRET else pltpu.with_memory_space_constraint(x, pltpu.HBM)


def sds(shape, dtype):
    return jax.ShapeDtypeStruct(shape, dtype)


def vout(shape, dtype):
    return sds(shape, dtype) if INTERPRET else pltpu.VMEM(shape, dtype)


def vm():
    return pl.BlockSpec(memory_space=pltpu.VMEM)


def sm():
    return pl.BlockSpec(memory_space=pltpu.SMEM)


def parts3(x):
    hi = x.astype(BF).astype(F32)
    rest = x - hi
    mid = rest.astype(BF).astype(F32)
    lo = rest - mid
    return hi, mid, lo


def norm_rows(h, gain):
    x = h.astype(F32)
    mean = jnp.mean(x, axis=-1, keepdims=True)
    xc = x - mean
    var = jnp.mean(xc * xc, axis=-1, keepdims=True)
    return (xc * lax.rsqrt(var + NORM_EPS) * gain).astype(BF)


def emit_rows(side, tiles, coords, r0, r1, g, cbuf):
    blocks = []
    for t in range(4):
        cbuf[t] = jnp.zeros((16, T), F32)
        for c in range(3):
            for k, part in enumerate(parts3(coords(c, t))):
                cbuf[t, c * 3 + k : c * 3 + k + 1, :] = part
        blocks.append(cbuf[t].astype(BF))
    for t in range(4):
        dst = r0 if t < 2 else r1
        dst[t % 2, 0:T, :] = tiles[t]
        dst[t % 2, T:PR, :] = blocks[t]
    for la in range(2):
        pick = side == 0
        g[la, 0:T, :] = jnp.where(pick, tiles[2 * la + 1], tiles[2 * la])
        g[la, T:PR, :] = jnp.where(pick, blocks[2 * la + 1], blocks[2 * la])


def first_body(side, h, p, gain, r0, r1, g, cbuf):
    tiles = [norm_rows(h[0, t // 2, t % 2], gain[...]) for t in range(4)]
    emit_rows(side[0], tiles, lambda c, t: own_rows(p, t)[c], r0, r1, g, cbuf)


def second_body(side, x, gain, r0, r1, g, h, p, cbuf):
    for t in range(4):
        for c in range(3):
            blk = x[4 * t + c, 32:40, :].astype(F32)
            p[0, c, t // 2, t % 2 : t % 2 + 1, :] = blk[0:1] + blk[1:2] + blk[2:3]
        for q in range(4):
            h[t, q * 32 : (q + 1) * 32, :] = x[4 * t + q, 0:32, :]
    tiles = [norm_rows(h[t], gain[...]) for t in range(4)]
    emit_rows(side[0], tiles, lambda c, t: own_rows(p, t)[c], r0, r1, g, cbuf)


def head_mask(e, shape):
    lane = lax.broadcasted_iota(jnp.int32, shape, 1)
    return (lane & (F - 1)) // HD == e


def origin(p):
    return [p[0, c, 0, 0:1, 0:1] for c in range(3)]


def project_kv(tile, n, rows, center, wkv, charge, kbuf, vbuf, jbuf, turned=False):
    kv = jnp.dot(tile, wkv, preferred_element_type=F32)
    k = kv[:, :F].astype(BF)
    kbuf[n] = kv[:, :F].T.astype(BF) if turned else k
    probe = lax.dot_general(charge, k, (((1,), (1,)), ((), ())), preferred_element_type=F32)[0:1]
    terms = [probe] + [probe * (rows[c] - center[c]) for c in range(3)]
    stack = [part for term in terms for part in parts3(term)] + [jnp.zeros((4, T), F32)]
    force = jnp.concatenate(stack, axis=0)
    force = jnp.concatenate([force] * HEADS, axis=0).T
    both = jnp.concatenate([kv[:, F:], force], axis=1).astype(BF)
    zero = jnp.zeros_like(both)
    for e in range(HEADS):
        vbuf[n, e * T : (e + 1) * T, :] = jnp.where(head_mask(e, both.shape), both, zero)
    jbuf[n] = jnp.concatenate(list(rows) + [jnp.zeros((5, T), F32)], axis=0)


def project_q(tile, m, wq, qbuf):
    q = jnp.dot(tile, wq, preferred_element_type=F32).astype(BF)
    q = q * jnp.asarray(0.125, BF)
    zero = jnp.zeros_like(q)
    for e in range(HEADS):
        qbuf[m, e * T : (e + 1) * T, :] = jnp.where(head_mask(e, q.shape), q, zero)


def geometry(mine, near, limit, i):
    mine = mine[i * ROWS : (i + 1) * ROWS, :]
    d = [mine[:, c : c + 1] - near[c : c + 1, :] for c in range(3)]
    r2 = d[0] * d[0] + d[1] * d[1] + d[2] * d[2]
    coefs = cos_half_coefs()
    poly = r2 * coefs[-1] + coefs[-2]
    for cf in coefs[-3::-1]:
        poly = poly * r2 + cf
    return r2, jnp.where(r2 < limit, poly * poly, 0.0).astype(BF)


def pair_terms(turned, m, n, limit, decays, qbuf, kbuf, vbuf, jbuf, ibuf, macc):
    near = jbuf[n]
    mine = ibuf[m]
    k = kbuf[n]
    parts = [geometry(mine, near, limit, i) for i in range(T // ROWS)]
    cut = jnp.concatenate([part[1] for part in parts], axis=0)
    ws = []
    size = 4 if turned else 2
    for group in range(HEADS // size):
        half = lax.dot_general(
            qbuf[m, group * size * T : (group + 1) * size * T, :],
            k,
            (((1,), (0 if turned else 1,)), ((), ())),
            preferred_element_type=F32,
        ).astype(BF)
        for s in range(size):
            e = group * size + s
            u = half[s * T : (s + 1) * T, :]
            power = jnp.concatenate([(part[0] * decays[e]).astype(BF) for part in parts], axis=0)
            ws.append((u + u * jnp.tanh(u)) * (jnp.exp2(power) * cut))
    macc[m] += jnp.dot(jnp.concatenate(ws, axis=1), vbuf[n], preferred_element_type=F32)


def visit(wide, slots, table, falloff, lo, hi, todo, qbuf, kbuf, vbuf, jbuf, ibuf, macc):
    count = jnp.int32(0)
    for t in range(4):
        for s in range(K):
            n = table[slots[t // 2, t % 2, s] + 1]
            todo[count] = (n - lo) * 4 + t
            count = count + jnp.where((n >= lo) & (n < hi), 1, 0)
    todo[count] = 0
    decays = [falloff[e] * (-LOG2E) for e in range(HEADS)]

    def step(i, carry):
        for s in range(wide):
            at = i * wide + s
            code = todo[jnp.minimum(at, count)]
            limit = jnp.where(at < count, 1.0, 0.0)
            n = code // 4
            pair_terms(
                wide == OWN_WIDE, code - n * 4, n, limit, decays, qbuf, kbuf, vbuf, jbuf, ibuf, macc
            )
        return carry

    lax.fori_loop(0, (count + wide - 1) // wide, step, 0)


def own_rows(p, t):
    return [p[0, c, t // 2, t % 2 : t % 2 + 1, :] for c in range(3)]


def own_columns(p, ibuf, t):
    ibuf[t] = jnp.concatenate(own_rows(p, t) + [jnp.zeros((5, T), F32)], axis=0).T


def own_body(
    slots, table, falloff, r0, r1, p, wqkv, charge, macc, qbuf, ibuf, todo, kbuf, vbuf, jbuf
):
    center = origin(p)
    for t in range(4):
        tile = (r0 if t < 2 else r1)[t % 2, 0:T, :]
        project_kv(
            tile, t, own_rows(p, t), center, wqkv[:, F:], charge_rows(charge), kbuf, vbuf, jbuf,
            True,
        )
        project_q(tile, t, wqkv[:, :F], qbuf)
        own_columns(p, ibuf, t)
        macc[t] = jnp.zeros((T, 2 * F), F32)
    visit(OWN_WIDE, slots, table, falloff, 0, 4, todo, qbuf, kbuf, vbuf, jbuf, ibuf, macc)


def project_halo(halo, p, wqkv, charge, kbuf, vbuf, jbuf):
    center = origin(p)
    for i, (src, a) in enumerate(halo):
        blk = src[a, T:PR, :].astype(F32)
        rows = [
            blk[3 * c : 3 * c + 1] + blk[3 * c + 1 : 3 * c + 2] + blk[3 * c + 2 : 3 * c + 3]
            for c in range(3)
        ]
        project_kv(
            src[a, 0:T, :], i, rows, center, wqkv[:, F:], charge_rows(charge), kbuf, vbuf, jbuf
        )


def edge_body(
    slots, table, falloff, p, qbuf, ibuf, up, down, gin, macc_in, wqkv, charge,
    macc, todo, kbuf, vbuf, jbuf,
):
    halo = [(up, 0), (up, 1), (down, 0), (down, 1), (gin, 0), (gin, 1)]
    project_halo(halo, p, wqkv, charge, kbuf, vbuf, jbuf)
    for t in range(4):
        macc[t] = macc_in[t]
    visit(WIDE, slots, table, falloff, 4, 10, todo, qbuf, kbuf, vbuf, jbuf, ibuf, macc)


def charge_rows(charge):
    return jnp.broadcast_to(charge[...].astype(F32), (16, F)).astype(BF)


def rest_body(
    last,
    slots, table, falloff, headw, levels, heat, p, qbuf, ibuf, h, jit, c0, c1,
    macc_in, wqkv, wo, charge,
    *refs,
):
    if last:
        hout, pout, fout = refs[:3]
        refs = refs[3:]
    else:
        xout = refs[0]
        refs = refs[1:]
    todo, kbuf, vbuf, jbuf, macc = refs
    center = origin(p)
    project_halo([(c0, 1), (c1, 0)], p, wqkv, charge, kbuf, vbuf, jbuf)
    for t in range(4):
        macc[t] = macc_in[t]
    visit(2, slots, table, falloff, 10, 12, todo, qbuf, kbuf, vbuf, jbuf, ibuf, macc)
    scale = JITTER * jnp.sqrt(jnp.full((1, T), levels[heat[0]], F32))
    for t in range(4):
        a, b = t // 2, t % 2
        message = (macc[t, :, :F] * MESSAGE_SCALE).astype(BF)
        mixed = jnp.dot(message, wo[...], preferred_element_type=F32)
        old = h[0, a, b] if len(h.shape) == 5 else h[t]
        updated = (old.astype(F32) + mixed).astype(BF)
        if last:
            hout[0, a, b] = updated
        else:
            for q in range(4):
                xout[4 * t + q, 0:32, :] = updated[q * 32 : (q + 1) * 32, :]
        terms = macc[t, :, F:].T
        total = terms[0:HD, :] * headw[0]
        for e in range(1, HEADS):
            total = total + terms[e * HD : (e + 1) * HD, :] * headw[e]
        sums = [total[3 * c : 3 * c + 1] + total[3 * c + 1 : 3 * c + 2] + total[3 * c + 2 : 3 * c + 3] for c in range(4)]
        for c, row in enumerate(own_rows(p, t)):
            force = ((row - center[c]) * sums[0] - sums[c + 1]) * FORCE_SCALE
            moved = row + DELTA * force + scale * jit[0, c, a, b : b + 1, :]
            if last:
                pout[0, c, a, b : b + 1, :] = moved
                fout[0, c, a, b : b + 1, :] = force
            else:
                xout[4 * t + c, 32:40, :] = jnp.concatenate(
                    list(parts3(moved)) + [jnp.zeros((5, T), F32)], axis=0
                ).astype(BF)
        if not last:
            xout[4 * t + 3, 32:40, :] = jnp.zeros((8, T), BF)


def route_body(partner, x, out):
    for r in range(16):
        out[r] = x[partner[r]]


def scratch(count):
    return [
        pltpu.SMEM((4 * K + 1,), jnp.int32),
        pltpu.VMEM((count, T, F), BF),
        pltpu.VMEM((count, HEADS * T, 2 * F), BF),
        pltpu.VMEM((count, 8, T), F32),
    ]


HSHAPE = (1, 2, 2, T, F)
PSHAPE = (1, 3, 2, 2, T)


def move(last, rows, p, h, jit, slots, consts):
    r0, r1, g = rows
    table = jnp.asarray(STORED, jnp.int32)
    wqkv, wo, charge, falloff, headw, levels, heat = consts
    gx = lax.axis_size("gx")
    swap = [(0, 1), (1, 0)]
    fwd = [(i, (i + 1) % gx) for i in range(gx)]
    bwd = [((i + 1) % gx, i) for i in range(gx)]
    gin = lax.ppermute(g, "gy", swap)
    up = near(lax.ppermute(r1, "gx", fwd))
    down = near(lax.ppermute(r0, "gx", bwd))
    sums = vout((4, T, 2 * F), F32)
    macc, qbuf, ibuf = call(
        own_body,
        "own",
        (sums, vout((4, HEADS * T, F), BF), vout((4, T, 8), F32)),
        [sm()] * 3 + [vm()] * 5,
        scratch(4),
    )(slots, table, falloff, near(r0), near(r1), p, wqkv, charge)
    gin, macc = lax.optimization_barrier((gin, macc))
    c0 = lax.ppermute(gin, "gx", fwd)
    c1 = lax.ppermute(gin, "gx", bwd)
    qbuf, ibuf = near(qbuf), near(ibuf)
    macc = call(edge_body, "edge", sums, [sm()] * 3 + [vm()] * 9, scratch(6))(
        slots, table, falloff, p, qbuf, ibuf, up, down, near(gin), near(macc), wqkv, charge
    )
    c0, c1, macc = lax.optimization_barrier((c0, c1, macc))
    if last:
        outs = (sds(HSHAPE, BF), sds(PSHAPE, F32), sds(PSHAPE, F32))
    else:
        outs = vout((16, XR, F), BF)
    return call(
        lambda *refs: rest_body(last, *refs),
        "rest",
        outs,
        [sm()] * 6 + [vm()] * 11,
        scratch(2) + [pltpu.VMEM((4, T, 2 * F), F32)],
    )(
        slots, table, falloff, headw, levels, heat, p, qbuf, ibuf, h, jit, near(c0), near(c1),
        near(macc), wqkv, wo, charge,
    )


def per_device(
    descriptors, locations, jit1, jit2, slots, levels, heat, partner,
    gain, wqkv, wo, charge, falloff, headw,
):
    gain = gain.reshape(1, F)
    charge = near(charge.reshape(1, F))
    wqkv = near(wqkv)
    wo = near(wo)
    side = lax.axis_index("gy").reshape(1).astype(jnp.int32)
    consts = (wqkv, wo, charge, falloff, headw, levels, heat)
    row = vout((2, PR, F), BF)
    rows = call(
        first_body, "first", (row, row, row), [sm()] + [vm()] * 3, [pltpu.VMEM((4, 16, T), F32)]
    )(side, far(descriptors), far(locations), far(gain))
    x = move(False, rows, near(locations), near(descriptors), near(jit1), slots, consts)
    x = lax.all_to_all(x, "rep", split_axis=0, concat_axis=0, tiled=True)
    x = call(route_body, "route", vout((16, XR, F), BF), [sm(), vm()])(partner, near(x))
    x = lax.all_to_all(x, "rep", split_axis=0, concat_axis=0, tiled=True)
    r0, r1, g, h1, p1 = call(
        second_body,
        "second",
        (row, row, row, vout((4, T, F), BF), vout(PSHAPE, F32)),
        [sm()] + [vm()] * 2,
        [pltpu.VMEM((4, 16, T), F32)],
    )(side, near(x), near(gain))
    return move(True, (r0, r1, g), near(p1), near(h1), near(jit2), slots, consts)


def solution(mesh):
    in_specs = (
        P("rep", "gx", "gy", None, None),
        P("rep", None, "gx", "gy", None),
        P("rep", None, "gx", "gy", None),
        P("rep", None, "gx", "gy", None),
        P("gx", "gy", None),
        P(),
        P("rep"),
        P(),
        P(),
        P(),
        P(),
        P(),
        P(),
        P(),
    )
    out_specs = (
        P("rep", "gx", "gy", None, None),
        P("rep", None, "gx", "gy", None),
        P("rep", None, "gx", "gy", None),
    )
    return jax.shard_map(
        per_device, mesh=mesh, in_specs=in_specs, out_specs=out_specs, check_vma=False
    )
```

```python
import math

import jax
import jax.numpy as jnp
from jax import lax
from jax.experimental import pallas as pl
from jax.experimental.pallas import tpu as pltpu
from jax.sharding import PartitionSpec as P

F = 128
HEADS = 8
HD = 16
T = 128
K = 6
PR = T + 16
XR = 40
NORM_EPS = 1e-05
DELTA = 0.1
JITTER = 0.05
MESSAGE_SCALE = 1.0 / 32.0
FORCE_SCALE = 1.0 / 16.0
LOG2E = 1.4426950408889634
ROWS = T
WIDE = 3
OWN_WIDE = 4
STORED = (-1, 10, 4, 5, 10, 8, 0, 1, 8, 9, 2, 3, 9, 11, 6, 7, 11)
INTERPRET = False

BF = jnp.bfloat16
F32 = jnp.float32


def cos_half_coefs():
    return (
        0.9999999997799036,
        -1.2337005342697012,
        0.2536693224722507,
        -0.020862687547626383,
        0.000917723882055615,
        -2.3824535481836604e-05,
    )


def call(body, name, out_shape, in_specs, scratch=()):
    many = isinstance(out_shape, tuple)
    out_specs = (vm(),) * len(out_shape) if many else vm()
    return pl.pallas_call(
        body,
        name=name,
        out_shape=out_shape,
        in_specs=in_specs,
        out_specs=out_specs,
        scratch_shapes=scratch,
        compiler_params=pltpu.CompilerParams(vmem_limit_bytes=20 * 1024 * 1024),
        interpret=INTERPRET,
    )


def near(x):
    return x if INTERPRET else pltpu.with_memory_space_constraint(x, pltpu.VMEM)


def far(x):
    return x if INTERPRET else pltpu.with_memory_space_constraint(x, pltpu.HBM)


def sds(shape, dtype):
    return jax.ShapeDtypeStruct(shape, dtype)


def vout(shape, dtype):
    return sds(shape, dtype) if INTERPRET else pltpu.VMEM(shape, dtype)


def vm():
    return pl.BlockSpec(memory_space=pltpu.VMEM)


def sm():
    return pl.BlockSpec(memory_space=pltpu.SMEM)


def parts3(x):
    hi = x.astype(BF).astype(F32)
    rest = x - hi
    mid = rest.astype(BF).astype(F32)
    lo = rest - mid
    return hi, mid, lo


def norm_rows(h, gain):
    x = h.astype(F32)
    mean = jnp.mean(x, axis=-1, keepdims=True)
    xc = x - mean
    var = jnp.mean(xc * xc, axis=-1, keepdims=True)
    return (xc * lax.rsqrt(var + NORM_EPS) * gain).astype(BF)


def emit_rows(side, tiles, coords, r0, r1, g, cbuf):
    blocks = []
    for t in range(4):
        cbuf[t] = jnp.zeros((16, T), F32)
        for c in range(3):
            for k, part in enumerate(parts3(coords(c, t))):
                cbuf[t, c * 3 + k : c * 3 + k + 1, :] = part
        blocks.append(cbuf[t].astype(BF))
    for t in range(4):
        dst = r0 if t < 2 else r1
        dst[t % 2, 0:T, :] = tiles[t]
        dst[t % 2, T:PR, :] = blocks[t]
    for la in range(2):
        pick = side == 0
        g[la, 0:T, :] = jnp.where(pick, tiles[2 * la + 1], tiles[2 * la])
        g[la, T:PR, :] = jnp.where(pick, blocks[2 * la + 1], blocks[2 * la])


def first_body(side, h, p, gain, r0, r1, g, cbuf):
    tiles = [norm_rows(h[0, t // 2, t % 2], gain[...]) for t in range(4)]
    emit_rows(side[0], tiles, lambda c, t: own_rows(p, t)[c], r0, r1, g, cbuf)


def second_body(side, x, gain, r0, r1, g, h, p, cbuf):
    for t in range(4):
        for c in range(3):
            blk = x[4 * t + c, 32:40, :].astype(F32)
            p[0, c, t // 2, t % 2 : t % 2 + 1, :] = blk[0:1] + blk[1:2] + blk[2:3]
        for q in range(4):
            h[t, q * 32 : (q + 1) * 32, :] = x[4 * t + q, 0:32, :]
    tiles = [norm_rows(h[t], gain[...]) for t in range(4)]
    emit_rows(side[0], tiles, lambda c, t: own_rows(p, t)[c], r0, r1, g, cbuf)


def head_mask(e, shape):
    lane = lax.broadcasted_iota(jnp.int32, shape, 1)
    return (lane & (F - 1)) // HD == e


def origin(p):
    return [p[0, c, 0, 0:1, 0:1] for c in range(3)]


def project_kv(tile, n, rows, center, wkv, charge, kbuf, vbuf, jbuf, turned=False):
    kv = jnp.dot(tile, wkv, preferred_element_type=F32)
    k = kv[:, :F]
    k = (k.T if turned else k).astype(BF)
    kbuf[n] = k
    probe = lax.dot_general(
        charge, k, (((1,), (0 if turned else 1,)), ((), ())), preferred_element_type=F32
    )[0:1]
    terms = [probe] + [probe * (rows[c] - center[c]) for c in range(3)]
    stack = [part for term in terms for part in parts3(term)] + [jnp.zeros((4, T), F32)]
    force = jnp.concatenate(stack, axis=0)
    force = jnp.concatenate([force] * HEADS, axis=0).T
    both = jnp.concatenate([kv[:, F:], force], axis=1).astype(BF)
    zero = jnp.zeros_like(both)
    for e in range(HEADS):
        vbuf[n, e * T : (e + 1) * T, :] = jnp.where(head_mask(e, both.shape), both, zero)
    jbuf[n] = jnp.concatenate(list(rows) + [jnp.zeros((5, T), F32)], axis=0)


def project_q(tile, m, wq, qbuf):
    q = jnp.dot(tile, wq, preferred_element_type=F32).astype(BF)
    q = q * jnp.asarray(0.125, BF)
    zero = jnp.zeros_like(q)
    for e in range(HEADS):
        qbuf[m, e * T : (e + 1) * T, :] = jnp.where(head_mask(e, q.shape), q, zero)


def geometry(mine, near, limit, i):
    mine = mine[i * ROWS : (i + 1) * ROWS, :]
    d = [mine[:, c : c + 1] - near[c : c + 1, :] for c in range(3)]
    r2 = d[0] * d[0] + d[1] * d[1] + d[2] * d[2]
    coefs = cos_half_coefs()
    poly = r2 * coefs[-1] + coefs[-2]
    for cf in coefs[-3::-1]:
        poly = poly * r2 + cf
    return r2, jnp.where(r2 < limit, poly * poly, 0.0).astype(BF)


def pair_terms(turned, m, n, limit, decays, qbuf, kbuf, vbuf, jbuf, ibuf, macc):
    near = jbuf[n]
    mine = ibuf[m]
    k = kbuf[n]
    parts = [geometry(mine, near, limit, i) for i in range(T // ROWS)]
    cut = jnp.concatenate([part[1] for part in parts], axis=0)
    ws = []
    size = 4 if turned else 2
    for group in range(HEADS // size):
        half = lax.dot_general(
            qbuf[m, group * size * T : (group + 1) * size * T, :],
            k,
            (((1,), (0 if turned else 1,)), ((), ())),
            preferred_element_type=F32,
        ).astype(BF)
        for s in range(size):
            e = group * size + s
            u = half[s * T : (s + 1) * T, :]
            power = jnp.concatenate([(part[0] * decays[e]).astype(BF) for part in parts], axis=0)
            ws.append((u + u * jnp.tanh(u)) * (jnp.exp2(power) * cut))
    macc[m] += jnp.dot(jnp.concatenate(ws, axis=1), vbuf[n], preferred_element_type=F32)


def visit(wide, slots, table, falloff, lo, hi, todo, qbuf, kbuf, vbuf, jbuf, ibuf, macc):
    count = jnp.int32(0)
    for t in range(4):
        for s in range(K):
            n = table[slots[t // 2, t % 2, s] + 1]
            todo[count] = (n - lo) * 4 + t
            count = count + jnp.where((n >= lo) & (n < hi), 1, 0)
    todo[count] = 0
    decays = [falloff[e] * (-LOG2E) for e in range(HEADS)]

    def step(i, carry):
        for s in range(wide):
            at = i * wide + s
            code = todo[jnp.minimum(at, count)]
            limit = jnp.where(at < count, 1.0, 0.0)
            n = code // 4
            pair_terms(
                wide > 2, code - n * 4, n, limit, decays, qbuf, kbuf, vbuf, jbuf, ibuf, macc
            )
        return carry

    lax.fori_loop(0, (count + wide - 1) // wide, step, 0)


def own_rows(p, t):
    return [p[0, c, t // 2, t % 2 : t % 2 + 1, :] for c in range(3)]


def own_columns(p, ibuf, t):
    ibuf[t] = jnp.concatenate(own_rows(p, t) + [jnp.zeros((5, T), F32)], axis=0).T


def own_body(
    slots, table, falloff, r0, r1, p, wqkv, charge, macc, qbuf, ibuf, todo, kbuf, vbuf, jbuf
):
    center = origin(p)
    for t in range(4):
        tile = (r0 if t < 2 else r1)[t % 2, 0:T, :]
        project_kv(
            tile, t, own_rows(p, t), center, wqkv[:, F:], charge_rows(charge), kbuf, vbuf, jbuf,
            True,
        )
        project_q(tile, t, wqkv[:, :F], qbuf)
        own_columns(p, ibuf, t)
        macc[t] = jnp.zeros((T, 2 * F), F32)
    visit(OWN_WIDE, slots, table, falloff, 0, 4, todo, qbuf, kbuf, vbuf, jbuf, ibuf, macc)


def project_halo(turned, halo, p, wqkv, charge, kbuf, vbuf, jbuf):
    center = origin(p)
    for i, (src, a) in enumerate(halo):
        blk = src[a, T:PR, :].astype(F32)
        rows = [
            blk[3 * c : 3 * c + 1] + blk[3 * c + 1 : 3 * c + 2] + blk[3 * c + 2 : 3 * c + 3]
            for c in range(3)
        ]
        project_kv(
            src[a, 0:T, :], i, rows, center, wqkv[:, F:], charge_rows(charge), kbuf, vbuf, jbuf,
            turned,
        )


def edge_body(
    slots, table, falloff, p, qbuf, ibuf, up, down, gin, macc_in, wqkv, charge,
    macc, todo, kbuf, vbuf, jbuf,
):
    halo = [(up, 0), (up, 1), (down, 0), (down, 1), (gin, 0), (gin, 1)]
    project_halo(True, halo, p, wqkv, charge, kbuf, vbuf, jbuf)
    for t in range(4):
        macc[t] = macc_in[t]
    visit(WIDE, slots, table, falloff, 4, 10, todo, qbuf, kbuf, vbuf, jbuf, ibuf, macc)


def charge_rows(charge):
    return jnp.broadcast_to(charge[...].astype(F32), (16, F)).astype(BF)


def rest_body(
    last,
    slots, table, falloff, headw, levels, heat, p, qbuf, ibuf, h, jit, c0, c1,
    macc_in, wqkv, wo, charge,
    *refs,
):
    if last:
        hout, pout, fout = refs[:3]
        refs = refs[3:]
    else:
        xout = refs[0]
        refs = refs[1:]
    todo, kbuf, vbuf, jbuf, macc = refs
    center = origin(p)
    project_halo(False, [(c0, 1), (c1, 0)], p, wqkv, charge, kbuf, vbuf, jbuf)
    for t in range(4):
        macc[t] = macc_in[t]
    visit(2, slots, table, falloff, 10, 12, todo, qbuf, kbuf, vbuf, jbuf, ibuf, macc)
    scale = JITTER * jnp.sqrt(jnp.full((1, T), levels[heat[0]], F32))
    for t in range(4):
        a, b = t // 2, t % 2
        message = (macc[t, :, :F] * MESSAGE_SCALE).astype(BF)
        mixed = jnp.dot(message, wo[...], preferred_element_type=F32)
        old = h[0, a, b] if len(h.shape) == 5 else h[t]
        updated = (old.astype(F32) + mixed).astype(BF)
        if last:
            hout[0, a, b] = updated
        else:
            for q in range(4):
                xout[4 * t + q, 0:32, :] = updated[q * 32 : (q + 1) * 32, :]
        terms = macc[t, :, F:].T
        total = terms[0:HD, :] * headw[0]
        for e in range(1, HEADS):
            total = total + terms[e * HD : (e + 1) * HD, :] * headw[e]
        sums = [total[3 * c : 3 * c + 1] + total[3 * c + 1 : 3 * c + 2] + total[3 * c + 2 : 3 * c + 3] for c in range(4)]
        for c, row in enumerate(own_rows(p, t)):
            force = ((row - center[c]) * sums[0] - sums[c + 1]) * FORCE_SCALE
            moved = row + DELTA * force + scale * jit[0, c, a, b : b + 1, :]
            if last:
                pout[0, c, a, b : b + 1, :] = moved
                fout[0, c, a, b : b + 1, :] = force
            else:
                xout[4 * t + c, 32:40, :] = jnp.concatenate(
                    list(parts3(moved)) + [jnp.zeros((5, T), F32)], axis=0
                ).astype(BF)
        if not last:
            xout[4 * t + 3, 32:40, :] = jnp.zeros((8, T), BF)


def route_body(partner, x, out):
    for r in range(16):
        out[r] = x[partner[r]]


def scratch(count):
    return [
        pltpu.SMEM((4 * K + 1,), jnp.int32),
        pltpu.VMEM((count, T, F), BF),
        pltpu.VMEM((count, HEADS * T, 2 * F), BF),
        pltpu.VMEM((count, 8, T), F32),
    ]


HSHAPE = (1, 2, 2, T, F)
PSHAPE = (1, 3, 2, 2, T)


def move(last, rows, p, h, jit, slots, consts):
    r0, r1, g = rows
    table = jnp.asarray(STORED, jnp.int32)
    wqkv, wo, charge, falloff, headw, levels, heat = consts
    gx = lax.axis_size("gx")
    swap = [(0, 1), (1, 0)]
    fwd = [(i, (i + 1) % gx) for i in range(gx)]
    bwd = [((i + 1) % gx, i) for i in range(gx)]
    gin = lax.ppermute(g, "gy", swap)
    up = near(lax.ppermute(r1, "gx", fwd))
    down = near(lax.ppermute(r0, "gx", bwd))
    sums = vout((4, T, 2 * F), F32)
    macc, qbuf, ibuf = call(
        own_body,
        "own",
        (sums, vout((4, HEADS * T, F), BF), vout((4, T, 8), F32)),
        [sm()] * 3 + [vm()] * 5,
        scratch(4),
    )(slots, table, falloff, near(r0), near(r1), p, wqkv, charge)
    gin, macc = lax.optimization_barrier((gin, macc))
    c0 = lax.ppermute(gin, "gx", fwd)
    c1 = lax.ppermute(gin, "gx", bwd)
    qbuf, ibuf = near(qbuf), near(ibuf)
    macc = call(edge_body, "edge", sums, [sm()] * 3 + [vm()] * 9, scratch(6))(
        slots, table, falloff, p, qbuf, ibuf, up, down, near(gin), near(macc), wqkv, charge
    )
    c0, c1, macc = lax.optimization_barrier((c0, c1, macc))
    if last:
        outs = (sds(HSHAPE, BF), sds(PSHAPE, F32), sds(PSHAPE, F32))
    else:
        outs = vout((16, XR, F), BF)
    return call(
        lambda *refs: rest_body(last, *refs),
        "rest",
        outs,
        [sm()] * 6 + [vm()] * 11,
        scratch(2) + [pltpu.VMEM((4, T, 2 * F), F32)],
    )(
        slots, table, falloff, headw, levels, heat, p, qbuf, ibuf, h, jit, near(c0), near(c1),
        near(macc), wqkv, wo, charge,
    )


def per_device(
    descriptors, locations, jit1, jit2, slots, levels, heat, partner,
    gain, wqkv, wo, charge, falloff, headw,
):
    gain = gain.reshape(1, F)
    charge = near(charge.reshape(1, F))
    wqkv = near(wqkv)
    wo = near(wo)
    side = lax.axis_index("gy").reshape(1).astype(jnp.int32)
    consts = (wqkv, wo, charge, falloff, headw, levels, heat)
    row = vout((2, PR, F), BF)
    rows = call(
        first_body, "first", (row, row, row), [sm()] + [vm()] * 3, [pltpu.VMEM((4, 16, T), F32)]
    )(side, far(descriptors), far(locations), far(gain))
    x = move(False, rows, near(locations), near(descriptors), near(jit1), slots, consts)
    x = lax.all_to_all(x, "rep", split_axis=0, concat_axis=0, tiled=True)
    x = call(route_body, "route", vout((16, XR, F), BF), [sm(), vm()])(partner, near(x))
    x = lax.all_to_all(x, "rep", split_axis=0, concat_axis=0, tiled=True)
    r0, r1, g, h1, p1 = call(
        second_body,
        "second",
        (row, row, row, vout((4, T, F), BF), vout(PSHAPE, F32)),
        [sm()] + [vm()] * 2,
        [pltpu.VMEM((4, 16, T), F32)],
    )(side, near(x), near(gain))
    return move(True, (r0, r1, g), near(p1), near(h1), near(jit2), slots, consts)


def solution(mesh):
    in_specs = (
        P("rep", "gx", "gy", None, None),
        P("rep", None, "gx", "gy", None),
        P("rep", None, "gx", "gy", None),
        P("rep", None, "gx", "gy", None),
        P("gx", "gy", None),
        P(),
        P("rep"),
        P(),
        P(),
        P(),
        P(),
        P(),
        P(),
        P(),
    )
    out_specs = (
        P("rep", "gx", "gy", None, None),
        P("rep", None, "gx", "gy", None),
        P("rep", None, "gx", "gy", None),
    )
    return jax.shard_map(
        per_device, mesh=mesh, in_specs=in_specs, out_specs=out_specs, check_vma=False
    )
```

```python
import math

import jax
import jax.numpy as jnp
from jax import lax
from jax.experimental import pallas as pl
from jax.experimental.pallas import tpu as pltpu
from jax.sharding import PartitionSpec as P

F = 128
HEADS = 8
HD = 16
T = 128
K = 6
PR = T + 16
XR = 40
NORM_EPS = 1e-05
DELTA = 0.1
JITTER = 0.05
MESSAGE_SCALE = 1.0 / 32.0
FORCE_SCALE = 1.0 / 16.0
LOG2E = 1.4426950408889634
ROWS = T
WIDE = 3
OWN_WIDE = 4
STORED = (-1, 10, 4, 5, 10, 8, 0, 1, 8, 9, 2, 3, 9, 11, 6, 7, 11)
INTERPRET = False

BF = jnp.bfloat16
F32 = jnp.float32


def cos_half_coefs():
    return (
        0.9999999997799036,
        -1.2337005342697012,
        0.2536693224722507,
        -0.020862687547626383,
        0.000917723882055615,
        -2.3824535481836604e-05,
    )


def call(body, name, out_shape, in_specs, scratch=()):
    many = isinstance(out_shape, tuple)
    out_specs = (vm(),) * len(out_shape) if many else vm()
    return pl.pallas_call(
        body,
        name=name,
        out_shape=out_shape,
        in_specs=in_specs,
        out_specs=out_specs,
        scratch_shapes=scratch,
        compiler_params=pltpu.CompilerParams(vmem_limit_bytes=20 * 1024 * 1024),
        interpret=INTERPRET,
    )


def near(x):
    return x if INTERPRET else pltpu.with_memory_space_constraint(x, pltpu.VMEM)


def far(x):
    return x if INTERPRET else pltpu.with_memory_space_constraint(x, pltpu.HBM)


def sds(shape, dtype):
    return jax.ShapeDtypeStruct(shape, dtype)


def vout(shape, dtype):
    return sds(shape, dtype) if INTERPRET else pltpu.VMEM(shape, dtype)


def vm():
    return pl.BlockSpec(memory_space=pltpu.VMEM)


def sm():
    return pl.BlockSpec(memory_space=pltpu.SMEM)


def parts3(x):
    hi = x.astype(BF).astype(F32)
    rest = x - hi
    mid = rest.astype(BF).astype(F32)
    lo = rest - mid
    return hi, mid, lo


def norm_rows(h, gain):
    x = h.astype(F32)
    mean = jnp.mean(x, axis=-1, keepdims=True)
    xc = x - mean
    var = jnp.mean(xc * xc, axis=-1, keepdims=True)
    return (xc * lax.rsqrt(var + NORM_EPS) * gain).astype(BF)


def emit_rows(side, tiles, coords, r0, r1, g, cbuf):
    blocks = []
    for t in range(4):
        cbuf[t] = jnp.zeros((16, T), F32)
        for c in range(3):
            for k, part in enumerate(parts3(coords(c, t))):
                cbuf[t, c * 3 + k : c * 3 + k + 1, :] = part
        blocks.append(cbuf[t].astype(BF))
    for t in range(4):
        dst = r0 if t < 2 else r1
        dst[t % 2, 0:T, :] = tiles[t]
        dst[t % 2, T:PR, :] = blocks[t]
    for la in range(2):
        pick = side == 0
        g[la, 0:T, :] = jnp.where(pick, tiles[2 * la + 1], tiles[2 * la])
        g[la, T:PR, :] = jnp.where(pick, blocks[2 * la + 1], blocks[2 * la])


def first_body(side, h, p, gain, r0, r1, g, cbuf):
    tiles = [norm_rows(h[0, t // 2, t % 2], gain[...]) for t in range(4)]
    emit_rows(side[0], tiles, lambda c, t: own_rows(p, t)[c], r0, r1, g, cbuf)


def second_body(side, x, gain, r0, r1, g, h, p, cbuf):
    for t in range(4):
        for c in range(3):
            blk = x[4 * t + c, 32:40, :].astype(F32)
            p[0, c, t // 2, t % 2 : t % 2 + 1, :] = blk[0:1] + blk[1:2] + blk[2:3]
        for q in range(4):
            h[t, q * 32 : (q + 1) * 32, :] = x[4 * t + q, 0:32, :]
    tiles = [norm_rows(h[t], gain[...]) for t in range(4)]
    emit_rows(side[0], tiles, lambda c, t: own_rows(p, t)[c], r0, r1, g, cbuf)


def head_mask(e, shape):
    lane = lax.broadcasted_iota(jnp.int32, shape, 1)
    return (lane & (F - 1)) // HD == e


def origin(p):
    return [p[0, c, 0, 0:1, 0:1] for c in range(3)]


def project_kv(tile, n, rows, center, wkv, charge, kbuf, vbuf, jbuf, turned=False):
    kv = jnp.dot(tile, wkv, preferred_element_type=F32)
    k = kv[:, :F]
    k = (k.T if turned else k).astype(BF)
    kbuf[n] = k
    probe = lax.dot_general(
        charge, k, (((1,), (0 if turned else 1,)), ((), ())), preferred_element_type=F32
    )[0:1]
    terms = [probe] + [probe * (rows[c] - center[c]) for c in range(3)]
    stack = [part for term in terms for part in parts3(term)] + [jnp.zeros((4, T), F32)]
    force = jnp.concatenate(stack, axis=0)
    force = jnp.concatenate([force] * HEADS, axis=0).T
    both = jnp.concatenate([kv[:, F:], force], axis=1).astype(BF)
    zero = jnp.zeros_like(both)
    for e in range(HEADS):
        vbuf[n, e * T : (e + 1) * T, :] = jnp.where(head_mask(e, both.shape), both, zero)
    jbuf[n] = jnp.concatenate(list(rows) + [jnp.zeros((5, T), F32)], axis=0)


def project_q(tile, m, wq, qbuf):
    q = jnp.dot(tile, wq, preferred_element_type=F32).astype(BF)
    q = q * jnp.asarray(0.125, BF)
    zero = jnp.zeros_like(q)
    for e in range(HEADS):
        qbuf[m, e * T : (e + 1) * T, :] = jnp.where(head_mask(e, q.shape), q, zero)


def geometry(mine, near, limit, i):
    mine = mine[i * ROWS : (i + 1) * ROWS, :]
    d = [mine[:, c : c + 1] - near[c : c + 1, :] for c in range(3)]
    r2 = d[0] * d[0] + d[1] * d[1] + d[2] * d[2]
    coefs = cos_half_coefs()
    poly = r2 * coefs[-1] + coefs[-2]
    for cf in coefs[-3::-1]:
        poly = poly * r2 + cf
    return r2, jnp.where(r2 < limit, poly * poly, 0.0).astype(BF)


def pair_terms(turned, m, n, limit, decays, qbuf, kbuf, vbuf, jbuf, ibuf, macc):
    near = jbuf[n]
    mine = ibuf[m]
    k = kbuf[n]
    parts = [geometry(mine, near, limit, i) for i in range(T // ROWS)]
    cut = jnp.concatenate([part[1] for part in parts], axis=0)
    ws = []
    size = 4 if turned else 2
    for group in range(HEADS // size):
        half = lax.dot_general(
            qbuf[m, group * size * T : (group + 1) * size * T, :],
            k,
            (((1,), (0 if turned else 1,)), ((), ())),
            preferred_element_type=F32,
        ).astype(BF)
        for s in range(size):
            e = group * size + s
            u = half[s * T : (s + 1) * T, :]
            power = jnp.concatenate([(part[0] * decays[e]).astype(BF) for part in parts], axis=0)
            ws.append((u + u * jnp.tanh(u)) * (jnp.exp2(power) * cut))
    macc[m] += jnp.dot(jnp.concatenate(ws, axis=1), vbuf[n], preferred_element_type=F32)


def visit(wide, slots, table, falloff, lo, hi, todo, qbuf, kbuf, vbuf, jbuf, ibuf, macc):
    count = jnp.int32(0)
    for t in range(4):
        for s in range(K):
            n = table[slots[t // 2, t % 2, s] + 1]
            todo[count] = (n - lo) * 4 + t
            count = count + jnp.where((n >= lo) & (n < hi), 1, 0)
    todo[count] = 0
    decays = [falloff[e] * (-LOG2E) for e in range(HEADS)]

    def step(i, carry):
        for s in range(wide):
            at = i * wide + s
            code = todo[jnp.minimum(at, count)]
            limit = jnp.where(at < count, 1.0, 0.0)
            n = code // 4
            pair_terms(
                wide == OWN_WIDE, code - n * 4, n, limit, decays, qbuf, kbuf, vbuf, jbuf, ibuf, macc
            )
        return carry

    lax.fori_loop(0, (count + wide - 1) // wide, step, 0)


def own_rows(p, t):
    return [p[0, c, t // 2, t % 2 : t % 2 + 1, :] for c in range(3)]


def own_columns(p, ibuf, t):
    ibuf[t] = jnp.concatenate(own_rows(p, t) + [jnp.zeros((5, T), F32)], axis=0).T


def own_body(
    slots, table, falloff, r0, r1, p, wqkv, charge, macc, qbuf, ibuf, todo, kbuf, vbuf, jbuf
):
    center = origin(p)
    for t in range(4):
        tile = (r0 if t < 2 else r1)[t % 2, 0:T, :]
        project_kv(
            tile, t, own_rows(p, t), center, wqkv[:, F:], charge_rows(charge), kbuf, vbuf, jbuf,
            True,
        )
        project_q(tile, t, wqkv[:, :F], qbuf)
        own_columns(p, ibuf, t)
        macc[t] = jnp.zeros((T, 2 * F), F32)
    visit(OWN_WIDE, slots, table, falloff, 0, 4, todo, qbuf, kbuf, vbuf, jbuf, ibuf, macc)


def project_halo(turned, halo, p, wqkv, charge, kbuf, vbuf, jbuf):
    center = origin(p)
    for i, (src, a) in enumerate(halo):
        blk = src[a, T:PR, :].astype(F32)
        rows = [
            blk[3 * c : 3 * c + 1] + blk[3 * c + 1 : 3 * c + 2] + blk[3 * c + 2 : 3 * c + 3]
            for c in range(3)
        ]
        project_kv(
            src[a, 0:T, :], i, rows, center, wqkv[:, F:], charge_rows(charge), kbuf, vbuf, jbuf,
            turned,
        )


def edge_body(
    slots, table, falloff, p, qbuf, ibuf, up, down, gin, macc_in, wqkv, charge,
    macc, todo, kbuf, vbuf, jbuf,
):
    halo = [(up, 0), (up, 1), (down, 0), (down, 1), (gin, 0), (gin, 1)]
    project_halo(False, halo, p, wqkv, charge, kbuf, vbuf, jbuf)
    for t in range(4):
        macc[t] = macc_in[t]
    visit(WIDE, slots, table, falloff, 4, 10, todo, qbuf, kbuf, vbuf, jbuf, ibuf, macc)


def charge_rows(charge):
    return jnp.broadcast_to(charge[...].astype(F32), (16, F)).astype(BF)


def rest_body(
    last,
    slots, table, falloff, headw, levels, heat, p, qbuf, ibuf, h, jit, c0, c1,
    macc_in, wqkv, wo, charge,
    *refs,
):
    if last:
        hout, pout, fout = refs[:3]
        refs = refs[3:]
    else:
        xout = refs[0]
        refs = refs[1:]
    todo, kbuf, vbuf, jbuf, macc = refs
    center = origin(p)
    project_halo(False, [(c0, 1), (c1, 0)], p, wqkv, charge, kbuf, vbuf, jbuf)
    for t in range(4):
        macc[t] = macc_in[t]
    visit(2, slots, table, falloff, 10, 12, todo, qbuf, kbuf, vbuf, jbuf, ibuf, macc)
    scale = JITTER * jnp.sqrt(jnp.full((1, T), levels[heat[0]], F32))
    for t in range(4):
        a, b = t // 2, t % 2
        message = (macc[t, :, :F] * MESSAGE_SCALE).astype(BF)
        mixed = jnp.dot(message, wo[...], preferred_element_type=F32)
        old = h[0, a, b] if len(h.shape) == 5 else h[t]
        updated = (old.astype(F32) + mixed).astype(BF)
        if last:
            hout[0, a, b] = updated
        else:
            for q in range(4):
                xout[4 * t + q, 0:32, :] = updated[q * 32 : (q + 1) * 32, :]
        terms = macc[t, :, F:].T
        total = terms[0:HD, :] * headw[0]
        for e in range(1, HEADS):
            total = total + terms[e * HD : (e + 1) * HD, :] * headw[e]
        sums = [total[3 * c : 3 * c + 1] + total[3 * c + 1 : 3 * c + 2] + total[3 * c + 2 : 3 * c + 3] for c in range(4)]
        for c, row in enumerate(own_rows(p, t)):
            force = ((row - center[c]) * sums[0] - sums[c + 1]) * FORCE_SCALE
            moved = row + DELTA * force + scale * jit[0, c, a, b : b + 1, :]
            if last:
                pout[0, c, a, b : b + 1, :] = moved
                fout[0, c, a, b : b + 1, :] = force
            else:
                xout[4 * t + c, 32:40, :] = jnp.concatenate(
                    list(parts3(moved)) + [jnp.zeros((5, T), F32)], axis=0
                ).astype(BF)
        if not last:
            xout[4 * t + 3, 32:40, :] = jnp.zeros((8, T), BF)


def route_body(partner, x, out):
    for r in range(16):
        out[r] = x[partner[r]]


def scratch(count):
    return [
        pltpu.SMEM((4 * K + 1,), jnp.int32),
        pltpu.VMEM((count, T, F), BF),
        pltpu.VMEM((count, HEADS * T, 2 * F), BF),
        pltpu.VMEM((count, 8, T), F32),
    ]


HSHAPE = (1, 2, 2, T, F)
PSHAPE = (1, 3, 2, 2, T)


def move(last, rows, p, h, jit, slots, consts):
    r0, r1, g = rows
    table = jnp.asarray(STORED, jnp.int32)
    wqkv, wo, charge, falloff, headw, levels, heat = consts
    gx = lax.axis_size("gx")
    swap = [(0, 1), (1, 0)]
    fwd = [(i, (i + 1) % gx) for i in range(gx)]
    bwd = [((i + 1) % gx, i) for i in range(gx)]
    gin = lax.ppermute(g, "gy", swap)
    up = near(lax.ppermute(r1, "gx", fwd))
    down = near(lax.ppermute(r0, "gx", bwd))
    sums = vout((4, T, 2 * F), F32)
    macc, qbuf, ibuf = call(
        own_body,
        "own",
        (sums, vout((4, HEADS * T, F), BF), vout((4, T, 8), F32)),
        [sm()] * 3 + [vm()] * 5,
        scratch(4),
    )(slots, table, falloff, near(r0), near(r1), p, wqkv, charge)
    gin, macc = lax.optimization_barrier((gin, macc))
    c0 = lax.ppermute(gin, "gx", fwd)
    c1 = lax.ppermute(gin, "gx", bwd)
    qbuf, ibuf = near(qbuf), near(ibuf)
    macc = call(edge_body, "edge", sums, [sm()] * 3 + [vm()] * 9, scratch(6))(
        slots, table, falloff, p, qbuf, ibuf, up, down, near(gin), near(macc), wqkv, charge
    )
    c0, c1, macc = lax.optimization_barrier((c0, c1, macc))
    if last:
        outs = (sds(HSHAPE, BF), sds(PSHAPE, F32), sds(PSHAPE, F32))
    else:
        outs = vout((16, XR, F), BF)
    return call(
        lambda *refs: rest_body(last, *refs),
        "rest",
        outs,
        [sm()] * 6 + [vm()] * 11,
        scratch(2) + [pltpu.VMEM((4, T, 2 * F), F32)],
    )(
        slots, table, falloff, headw, levels, heat, p, qbuf, ibuf, h, jit, near(c0), near(c1),
        near(macc), wqkv, wo, charge,
    )


def per_device(
    descriptors, locations, jit1, jit2, slots, levels, heat, partner,
    gain, wqkv, wo, charge, falloff, headw,
):
    gain = gain.reshape(1, F)
    charge = near(charge.reshape(1, F))
    wqkv = near(wqkv)
    wo = near(wo)
    side = lax.axis_index("gy").reshape(1).astype(jnp.int32)
    consts = (wqkv, wo, charge, falloff, headw, levels, heat)
    row = vout((2, PR, F), BF)
    rows = call(
        first_body, "first", (row, row, row), [sm()] + [vm()] * 3, [pltpu.VMEM((4, 16, T), F32)]
    )(side, far(descriptors), far(locations), far(gain))
    x = move(False, rows, near(locations), near(descriptors), near(jit1), slots, consts)
    x = lax.all_to_all(x, "rep", split_axis=0, concat_axis=0, tiled=True)
    x = call(route_body, "route", vout((16, XR, F), BF), [sm(), vm()])(partner, near(x))
    x = lax.all_to_all(x, "rep", split_axis=0, concat_axis=0, tiled=True)
    r0, r1, g, h1, p1 = call(
        second_body,
        "second",
        (row, row, row, vout((4, T, F), BF), vout(PSHAPE, F32)),
        [sm()] + [vm()] * 2,
        [pltpu.VMEM((4, 16, T), F32)],
    )(side, near(x), near(gain))
    return move(True, (r0, r1, g), near(p1), near(h1), near(jit2), slots, consts)


def solution(mesh):
    in_specs = (
        P("rep", "gx", "gy", None, None),
        P("rep", None, "gx", "gy", None),
        P("rep", None, "gx", "gy", None),
        P("rep", None, "gx", "gy", None),
        P("gx", "gy", None),
        P(),
        P("rep"),
        P(),
        P(),
        P(),
        P(),
        P(),
        P(),
        P(),
    )
    out_specs = (
        P("rep", "gx", "gy", None, None),
        P("rep", None, "gx", "gy", None),
        P("rep", None, "gx", "gy", None),
    )
    return jax.shard_map(
        per_device, mesh=mesh, in_specs=in_specs, out_specs=out_specs, check_vma=False
    )
```
